32 devices in a mesh: cells: 16 (over z, x, core), src: 2 (over y).
Axes of the slice: x: 2, y: 2, z: 4, core: 2. Of those that a mesh axis runs over, the one named last changes fastest.
Arguments:
- conductivity: float32 [64, 1024], P('cells'), may hold values from 0.2 to 5
- prev_fields: bfloat16 [1024, 64, 1024], P('src', 'cells'), may hold values from -6 to 6
- electrodes: int32 [1024, 2], P('src'), may hold values from 0 to 65535, as said below
- data_weight: bfloat16 [1024, 1024], replicated, may hold values from -3 to 4
Outputs:
- potentials: bfloat16 [1024, 64, 1024], P('src', 'cells')
- gradient: float32 [64, 1024], P('cells', 'src')
The draws below stay inside these ranges and needn't reach their ends.
Inputs may be any that keep to these rules, and one draw needn't show every extreme that they name: `electrodes`: in each row the two cells differ.
All inputs are finite; a program needn't handle non-finite values.
Results may differ from the reference program's by a relative error of at most 0.0034.
Values may be sent and summed in bfloat16 or wider, within the bound.
No kernel may reach another device: no remote copies, remote signals or barrier semaphores. Data moves between devices by JAX's collectives and lax.ppermute only.
A program may use at most 128 MiB of HBM per device.

```python
import math
import jax
import jax.numpy as jnp
from jax import lax

S = 1024
NX = 32
NY = 32
ITERS = 2
NZ = 64


def draw_electrodes(key, part):
    first_key, second_key = jax.random.split(jax.random.fold_in(key, 5))
    ncell = NZ * NX * NY
    source_cell = jax.random.randint(first_key, (S,), 0, ncell, dtype=jnp.int32)
    stride = jax.random.randint(second_key, (S,), 1, ncell, dtype=jnp.int32)
    sink_cell = (source_cell + stride) % ncell
    return jnp.stack([source_cell, sink_cell], axis=1).astype(jnp.int32)


def draw_data_weight(key, part):
    first_key, second_key = jax.random.split(jax.random.fold_in(key, 11))
    scales = jnp.exp(jax.random.uniform(first_key, (S,), jnp.float32, math.log(0.1), 0.0))
    spread = jnp.clip(jax.random.normal(second_key, (S, S), jnp.float32), -4.0, 4.0)
    weights = jnp.diag(scales) + spread * (4.0 / math.sqrt(S))
    return weights.astype(jnp.bfloat16)


def level_of(own_key, dims, shards, low, high):
    def one(dim, shards_of):
        steps = jax.random.uniform(jax.random.fold_in(jax.random.fold_in(own_key, 6), dim), (shards_of,), jnp.float32, low / len(shards), high / len(shards))
        return jnp.repeat(jnp.exp(steps), dims[dim] // shards_of).reshape((-1,) + (1,) * (len(dims) - dim - 1))

    factor_of = one(*shards[0])
    for cut in shards[1:]:
        factor_of = factor_of * one(*cut)
    return factor_of


def gaussian(own_key, shape, scale, bound, cuts=(), kind=jnp.bfloat16):
    drawn = scale * jax.random.normal(own_key, shape, jnp.float32)
    if cuts:
        drawn = drawn * level_of(own_key, shape, cuts, -0.22, 0.18)
    return jnp.clip(drawn, -bound, bound).astype(kind)


def setup_inputs(seed: int = 0) -> dict:
    key_list = jax.random.split(jax.random.key(seed), 5)
    conductivity = jnp.clip(jnp.exp(math.log(5.0) - 3.218876 * jax.random.uniform(key_list[0], (NZ, NX * NY), jnp.float32) ** level_of(key_list[0], (NZ, NX * NY), ((0, 16),), -0.2, 0.2)), 0.2, 5.0)
    prev_fields = gaussian(key_list[1], (S, NZ, NX * NY), 1.0, 6.0, ((0, 2), (1, 16)))
    electrodes = draw_electrodes(jax.random.fold_in(key_list[4], 71), 0)
    data_weight = draw_data_weight(jax.random.fold_in(key_list[4], 71), 0)
    return {"conductivity": conductivity, "prev_fields": prev_fields, "electrodes": electrodes, "data_weight": data_weight}


relaxation = 2.0 / 3.0
current = 4.0


def shift_last(values, offset):
    if offset > 0:
        padding = jnp.zeros(values.shape[:-1] + (offset,), values.dtype)
        return jnp.concatenate([values[..., offset:], padding], axis=-1)
    padding = jnp.zeros(values.shape[:-1] + (-offset,), values.dtype)
    return jnp.concatenate([padding, values[..., :offset]], axis=-1)


def column_masks(length, row_len):
    column = jnp.arange(length, dtype=jnp.int32) % row_len
    return (column != row_len - 1).astype(jnp.float32), (column != 0).astype(jnp.float32)


def coefficients(sigma_pad, row_len):
    sigma = sigma_pad[1:-1]
    upper_mask, lower_mask = column_masks(sigma.shape[-1], row_len)
    z_plus = 0.5 * (sigma + sigma_pad[2:])
    z_minus = 0.5 * (sigma + sigma_pad[:-2])
    y_plus = 0.5 * (sigma + shift_last(sigma, 1) * upper_mask)
    y_minus = 0.5 * (sigma + shift_last(sigma, -1) * lower_mask)
    x_plus = 0.5 * (sigma + shift_last(sigma, row_len))
    x_minus = 0.5 * (sigma + shift_last(sigma, -row_len))
    diagonal = z_plus + z_minus + y_plus + y_minus + x_plus + x_minus
    return (z_plus, z_minus, y_plus, y_minus, x_plus, x_minus, diagonal, upper_mask, lower_mask)


def relax(fields_pad, source, coeffs, row_len):
    z_plus, z_minus, y_plus, y_minus, x_plus, x_minus, diagonal, upper_mask, lower_mask = coeffs
    fields = fields_pad[:, 1:-1]
    applied = diagonal * fields - z_plus * fields_pad[:, 2:] - z_minus * fields_pad[:, :-2]
    applied = applied - y_plus * (shift_last(fields, 1) * upper_mask) - y_minus * (shift_last(fields, -1) * lower_mask)
    applied = applied - x_plus * shift_last(fields, row_len) - x_minus * shift_last(fields, -row_len)
    return fields + relaxation * (source - applied) / diagonal


def differences(planes, above, beside, row_len):
    upper_mask, lower_mask = column_masks(planes.shape[-1], row_len)
    along_x = jnp.concatenate([planes[..., row_len:], beside], axis=-1)
    along_y = shift_last(planes, 1) * upper_mask
    along_z = jnp.concatenate([planes[:, 1:], above], axis=1)
    return tuple((shifted - planes).astype(jnp.bfloat16) for shifted in (along_x, along_y, along_z))


def weigh(diffs, data_weight):
    count = data_weight.shape[0]
    total = jnp.zeros(diffs[0].shape[1:], jnp.float32)
    for block in diffs:
        flat = block.reshape(count, -1)
        mixed = jnp.dot(data_weight, flat, preferred_element_type=jnp.float32)
        total = total + jnp.sum(flat.astype(jnp.float32) * mixed, axis=0).reshape(total.shape)
    return total / count


def reference(conductivity, prev_fields, electrodes, data_weight):
    ncell = NZ * NX * NY
    sigma_pad = jnp.pad(conductivity, ((1, 1), (0, 0)))
    coeffs = coefficients(sigma_pad, NY)
    width = min(128, S)
    cell_ids = jnp.arange(ncell, dtype=jnp.int32)

    def solve_block(inputs):
        start_fields, pairs = inputs
        source = current * ((cell_ids[None, :] == pairs[:, 0:1]).astype(jnp.float32)
                            - (cell_ids[None, :] == pairs[:, 1:2]).astype(jnp.float32))
        source = source.reshape(width, NZ, NX * NY)
        fields = start_fields.astype(jnp.float32)
        for sweep in range(ITERS):
            fields_pad = jnp.pad(fields, ((0, 0), (1, 1), (0, 0)))
            fields = relax(fields_pad, source, coeffs, NY)
        return fields.astype(jnp.bfloat16)

    blocks = lax.map(solve_block, (prev_fields.reshape(S // width, width, NZ, NX * NY),
                                   electrodes.reshape(S // width, width, 2)))
    potentials = blocks.reshape(S, NZ, NX * NY)
    padded = jnp.pad(potentials, ((0, 0), (0, 1), (0, 0)))

    def plane_gradient(level):
        slab = lax.dynamic_slice_in_dim(padded, level, 2, 1).astype(jnp.float32)
        beside = jnp.zeros((S, 1, NY), jnp.float32)
        return weigh(differences(slab[:, :1], slab[:, 1:], beside, NY), data_weight)

    gradient = lax.map(plane_gradient, jnp.arange(NZ, dtype=jnp.int32)).reshape(NZ, NX * NY)
    return potentials, gradient
```

```python
import functools

import jax
import jax.numpy as jnp
from jax import lax
from jax.experimental import pallas as pl
from jax.experimental.pallas import tpu as pltpu
from jax.sharding import PartitionSpec as P

NY = 32
current = 4.0
LANES = 128
GROUP = 16
ROWS = 32
UNIT = 128
LOW = 2
HIGH = 3


def neighbours(axis, step):
    count = lax.axis_size(axis)
    return [(i, i + step) for i in range(count) if 0 <= i + step < count]


def shift_last(values, offset):
    if offset > 0:
        padding = jnp.zeros(values.shape[:-1] + (offset,), values.dtype)
        return jnp.concatenate([values[..., offset:], padding], axis=-1)
    padding = jnp.zeros(values.shape[:-1] + (-offset,), values.dtype)
    return jnp.concatenate([padding, values[..., :offset]], axis=-1)


def stencil_coefficients(conductivity, first_plane, planes_total):
    depth, cells = conductivity.shape
    low = lax.ppermute(conductivity[depth - LOW :], "cells", neighbours("cells", 1))
    high = lax.ppermute(conductivity[:HIGH], "cells", neighbours("cells", -1))
    padded = jnp.concatenate([low, conductivity, high], axis=0)
    sigma = padded[1:-1]
    column = jnp.arange(cells, dtype=jnp.int32)
    upper = (column % NY != NY - 1).astype(jnp.float32)
    lower = (column % NY != 0).astype(jnp.float32)
    plane = first_plane - 1 + jnp.arange(sigma.shape[0], dtype=jnp.int32)
    inside = ((plane >= 0) & (plane < planes_total))[:, None]
    z_plus = 0.5 * (sigma + padded[2:])
    z_minus = 0.5 * (sigma + padded[:-2])
    y_plus = 0.5 * (sigma + shift_last(sigma, 1) * upper)
    y_minus = 0.5 * (sigma + shift_last(sigma, -1) * lower)
    x_plus = 0.5 * (sigma + shift_last(sigma, NY))
    x_minus = 0.5 * (sigma + shift_last(sigma, -NY))
    diagonal = z_plus + z_minus + y_plus + y_minus + x_plus + x_minus
    scale = jnp.where(inside, 2.0 / jnp.where(inside, diagonal, 1.0), 0.0)
    rows = [
        z_plus * scale,
        z_minus * scale,
        y_plus * scale * upper,
        y_minus * scale * lower,
        x_plus * scale * (column < cells - NY),
        x_minus * scale * (column >= NY),
        current * scale,
        jnp.zeros_like(scale),
    ]
    return jnp.stack(rows, axis=1)


def lane_index(shape):
    return lax.broadcasted_iota(jnp.int32, shape, 1)


def sweep_kernel(depth, count, band, place_ref, own_ref, low_ref, high_ref, coef_ref, elec_ref, *refs):
    refs = refs[-(count + 6) :]
    pot_ref, outs, (first, second, extra, final) = refs[0], refs[1 : count + 1], refs[count + 1 : count + 5]
    elec_b = refs[count + 5]
    rows, _, cells = own_ref.shape
    tiles = cells // LANES
    first[0:LOW] = low_ref[...].astype(jnp.float32)
    first[LOW : LOW + depth] = jnp.swapaxes(own_ref[...].astype(jnp.float32), 0, 1)
    first[LOW + depth :] = high_ref[...].astype(jnp.float32)
    elec_b[0] = jnp.broadcast_to(elec_ref[:, 0:1], (rows, LANES))
    elec_b[1] = jnp.broadcast_to(elec_ref[:, 1:2], (rows, LANES))
    lane = lane_index((GROUP, LANES))
    left = lane < LANES - NY
    right = lane >= NY
    groups = rows // GROUP

    def spread(row):
        return jnp.broadcast_to(row, (GROUP, LANES))

    def stencil(source, plane, coef_plane, at):
        centre = [source[plane, at, pl.ds(v * LANES, LANES)] for v in range(tiles)]
        ahead = [pltpu.roll(c, LANES - NY, 1) for c in centre]
        behind = [pltpu.roll(c, NY, 1) for c in centre]
        result = []
        for v in range(tiles):
            lanes = pl.ds(v * LANES, LANES)

            def coef(kind):
                return spread(coef_ref[coef_plane, kind : kind + 1, lanes])

            x_plus = ahead[v] if v == tiles - 1 else jnp.where(left, ahead[v], ahead[v + 1])
            x_minus = behind[v] if v == 0 else jnp.where(right, behind[v], behind[v - 1])
            total = centre[v] + coef(0) * source[plane + 1, at, lanes]
            side = coef(1) * source[plane - 1, at, lanes]
            total = total + coef(2) * pltpu.roll(centre[v], LANES - 1, 1)
            side = side + coef(3) * pltpu.roll(centre[v], 1, 1)
            total = total + coef(4) * x_plus
            side = side + coef(5) * x_minus
            result.append(total + side)
        return result

    def relax_first(step, carry):
        plane, group = step // groups, step % groups
        at = pl.ds(pl.multiple_of(group * GROUP, GROUP), GROUP)
        sums = stencil(first, plane + 1, plane, at)
        base = place_ref[1] + (plane - 1) * cells
        plus = elec_b[0, at, :] - base
        minus = elec_b[1, at, :] - base
        for v in range(tiles):
            lanes = pl.ds(v * LANES, LANES)
            strength = spread(coef_ref[plane, 6:7, lanes])
            here = lane + v * LANES
            added = jnp.where(plus == here, strength, jnp.where(minus == here, -strength, 0.0))
            extra[plane, at, lanes] = added
            second[plane, at, lanes] = sums[v] + added
        return carry

    lax.fori_loop(0, (depth + HIGH) * groups, relax_first, 0)

    def relax_second(step, carry):
        plane, group = step // groups, step % groups
        at = pl.ds(pl.multiple_of(group * GROUP, GROUP), GROUP)
        sums = stencil(second, plane + 1, plane + 1, at)
        for v in range(tiles):
            lanes = pl.ds(v * LANES, LANES)
            value = (sums[v] + 3.0 * extra[plane + 1, at, lanes]) * (1.0 / 9.0)
            final[plane, at, lanes] = value.astype(jnp.bfloat16)
        return carry

    lax.fori_loop(0, (depth + 1) * groups, relax_second, 0)
    pot_ref[...] = jnp.swapaxes(final[0:depth].astype(jnp.float32), 0, 1).astype(jnp.bfloat16)

    wide = lane_index((rows, LANES))
    for r in range(count):
        out = outs[r]
        target = lax.rem(place_ref[0] + r, count)
        start = pl.multiple_of(target * band, LANES)
        for plane in range(depth + 1):
            out[:, plane * band : (plane + 1) * band] = final[plane, :, pl.ds(start, band)]
        after = jnp.minimum(target + 1, count - 1)
        after_start = pl.multiple_of(after * band, LANES)
        kept = (target < count - 1).astype(jnp.float32)
        for piece in range(beside_width(depth) // LANES):
            packed = jnp.zeros((rows, LANES), jnp.float32)
            for slot in range(LANES // NY):
                plane = piece * (LANES // NY) + slot
                if plane < depth:
                    row = final[plane, :, pl.ds(after_start, LANES)].astype(jnp.float32)
                    row = pltpu.roll(row, slot * NY, 1) if slot else row
                    mine = (wide >= slot * NY) & (wide < (slot + 1) * NY)
                    packed = jnp.where(mine, row, packed)
            begin = (depth + 1) * band + piece * LANES
            out[:, begin : begin + LANES] = (packed * kept).astype(jnp.bfloat16)


def beside_width(depth):
    return -(-depth * NY // LANES) * LANES


def sweep(place, own, low, high, coefs, electrodes, before, begin, size, count, band):
    total, depth, cells = own.shape
    width = (depth + 1) * band + beside_width(depth)
    block = begin // ROWS
    in_specs = [
        pl.BlockSpec((ROWS, depth, cells), lambda i, place: (i + block, 0, 0)),
        pl.BlockSpec((LOW, ROWS, cells), lambda i, place: (0, i, 0)),
        pl.BlockSpec((HIGH, ROWS, cells), lambda i, place: (0, i, 0)),
        pl.BlockSpec(coefs.shape, lambda i, place: (0, 0, 0)),
        pl.BlockSpec((ROWS, 2), lambda i, place: (i + block, 0)),
    ]
    args = [place, own, low, high, coefs, electrodes]
    aliases = {}
    if before is not None:
        in_specs.append(pl.BlockSpec(memory_space=pl.ANY))
        args.append(before)
        aliases = {6: 0}
    planes = depth + HIGH
    flops = size * cells * planes * 40
    return pl.pallas_call(
        functools.partial(sweep_kernel, depth, count, band),
        grid_spec=pltpu.PrefetchScalarGridSpec(
            num_scalar_prefetch=1,
            grid=(size // ROWS,),
            in_specs=in_specs,
            out_specs=[pl.BlockSpec((ROWS, depth, cells), lambda i, place: (i + block, 0, 0))]
            + [pl.BlockSpec((ROWS, width), lambda i, place: (i, 0))] * count,
            scratch_shapes=[
                pltpu.VMEM((LOW + depth + HIGH, ROWS, cells), jnp.float32),
                pltpu.VMEM((planes, ROWS, cells), jnp.float32),
                pltpu.VMEM((planes, ROWS, cells), jnp.float32),
                pltpu.VMEM((depth + 1, ROWS, cells), jnp.bfloat16),
                pltpu.VMEM((2, ROWS, LANES), jnp.int32),
            ],
        ),
        out_shape=[jax.ShapeDtypeStruct(own.shape, jnp.bfloat16)]
        + [jax.ShapeDtypeStruct((size, width), jnp.bfloat16)] * count,
        input_output_aliases=aliases,
        compiler_params=pltpu.CompilerParams(vmem_limit_bytes=24 * 2**20),
        cost_estimate=pl.CostEstimate(
            flops=flops, bytes_accessed=size * cells * 2 * (3 * depth + LOW + HIGH), transcendentals=0
        ),
        name="sweep",
    )(*args)


def fold_kernel(count, per, place_ref, weight_ref, out_ref):
    total = count * per

    def where_is(block):
        holder = lax.rem(place_ref[0] + count - lax.rem(block, count), count)
        return pl.multiple_of((holder * per + lax.div(block, count)) * UNIT, UNIT)

    for q in range(total):
        here = where_is(q)
        chunk = q // count
        rows = pl.ds(q * UNIT, UNIT)

        def folded(other, carry):
            there = where_is(other)
            straight = weight_ref[pl.ds(here, UNIT), pl.ds(there, UNIT)].astype(jnp.float32)
            turned = weight_ref[pl.ds(there, UNIT), pl.ds(here, UNIT)].astype(jnp.float32)
            columns = pl.ds(pl.multiple_of(other * UNIT, UNIT), UNIT)
            out_ref[rows, columns] = (straight + turned.T).astype(jnp.bfloat16)
            return carry

        if chunk:
            lax.fori_loop(0, chunk * count, folded, 0)
        for other in range(chunk * count, (chunk + 1) * count):
            there = where_is(other)
            out_ref[rows, other * UNIT : (other + 1) * UNIT] = weight_ref[
                pl.ds(here, UNIT), pl.ds(there, UNIT)
            ]
        if chunk + 1 < per:
            out_ref[rows, (chunk + 1) * count * UNIT :] = jnp.zeros(
                (UNIT, (per - chunk - 1) * count * UNIT), jnp.bfloat16
            )


def fold(place, weight, count, per):
    return pl.pallas_call(
        functools.partial(fold_kernel, count, per),
        grid_spec=pltpu.PrefetchScalarGridSpec(
            num_scalar_prefetch=1,
            grid=(1,),
            in_specs=[pl.BlockSpec(weight.shape, lambda i, place: (0, 0))],
            out_specs=pl.BlockSpec(weight.shape, lambda i, place: (0, 0)),
        ),
        out_shape=jax.ShapeDtypeStruct(weight.shape, jnp.bfloat16),
        compiler_params=pltpu.CompilerParams(vmem_limit_bytes=24 * 2**20),
        cost_estimate=pl.CostEstimate(
            flops=weight.size, bytes_accessed=weight.size * 4, transcendentals=0
        ),
        name="fold",
    )(place, weight)


def weigh_kernel(depth, band, pieces, row_start, block_rows, scale, weight_ref, *refs):
    piece_refs = refs[:pieces]
    before_ref, out_ref, held, mixed, partial, sems = refs[pieces:]
    step = pl.program_id(0)
    width = held.shape[1]
    tiles = band // LANES

    @pl.when(step == 0)
    def _():
        at = 0
        copies = []
        for i, piece in enumerate(piece_refs):
            size = piece.shape[0]
            copies.append(pltpu.make_async_copy(piece, held.at[pl.ds(at, size)], sems.at[i]))
            copies[-1].start()
            at += size
        for copy in copies:
            copy.wait()
        partial[...] = before_ref[...]

    mixed[...] = jnp.dot(
        weight_ref[:, : held.shape[0]], held[...], preferred_element_type=jnp.float32
    )
    lane = lane_index((GROUP, LANES))
    left = lane < LANES - NY
    inner = jnp.where(lax.rem(lane, NY) != NY - 1, 1.0, 0.0)
    base = row_start + step * block_rows

    for plane in range(depth):
        beside_tile = (depth + 1) * band + (plane * NY // LANES) * LANES
        turn = (LANES - NY - plane * NY) % LANES

        def rows_of(group, totals):
            at = pl.ds(pl.multiple_of(group * GROUP, GROUP), GROUP)
            at_held = pl.ds(pl.multiple_of(base + group * GROUP, GROUP), GROUP)

            def read(column):
                lanes = pl.ds(column, LANES)
                return held[at_held, lanes].astype(jnp.float32), mixed[at, lanes]

            centre = [read(plane * band + t * LANES) for t in range(tiles)]
            above = [read((plane + 1) * band + t * LANES) for t in range(tiles)]
            ahead = [tuple(pltpu.roll(c, LANES - NY, 1) for c in pair) for pair in centre]
            ahead.append(tuple(pltpu.roll(c, turn, 1) if turn else c for c in read(beside_tile)))
            result = []
            for t in range(tiles):
                value, product = centre[t]
                total = (above[t][0] - value) * (above[t][1] - product)
                total = total + (jnp.where(left, ahead[t][0], ahead[t + 1][0]) - value) * (
                    jnp.where(left, ahead[t][1], ahead[t + 1][1]) - product
                )
                total = total + (pltpu.roll(value, LANES - 1, 1) * inner - value) * (
                    pltpu.roll(product, LANES - 1, 1) * inner - product
                )
                result.append(totals[t] + (total[:8] + total[8:]))
            return tuple(result)

        rows = pl.ds(plane * 8, 8)
        start = tuple(partial[rows, t * LANES : (t + 1) * LANES] for t in range(tiles))
        sums = lax.fori_loop(0, block_rows // GROUP, rows_of, start)
        for t in range(tiles):
            partial[rows, t * LANES : (t + 1) * LANES] = sums[t]

    @pl.when(step == pl.num_programs(0) - 1)
    def _():
        if scale is None:
            out_ref[...] = partial[...]
        else:
            for plane in range(depth):
                total = jnp.sum(partial[plane * 8 : plane * 8 + 8, :], axis=0, keepdims=True)
                out_ref[plane : plane + 1, :] = total * scale


def weigh(weight, pieces, before, row_start, rows, depth, band, scale):
    width = pieces[0].shape[1]
    held = sum(piece.shape[0] for piece in pieces)
    block_rows = UNIT
    first = row_start // block_rows
    out = (depth, band) if scale is not None else (depth * 8, band)
    return pl.pallas_call(
        functools.partial(weigh_kernel, depth, band, len(pieces), row_start, block_rows, scale),
        grid=(rows // block_rows,),
        in_specs=[pl.BlockSpec((block_rows, weight.shape[1]), lambda i: (i + first, 0))]
        + [pl.BlockSpec(memory_space=pl.ANY)] * len(pieces)
        + [pl.BlockSpec((depth * 8, band), lambda i: (0, 0))],
        out_specs=pl.BlockSpec(out, lambda i: (0, 0)),
        out_shape=jax.ShapeDtypeStruct(out, jnp.float32),
        scratch_shapes=[
            pltpu.VMEM((held, width), jnp.bfloat16),
            pltpu.VMEM((block_rows, width), jnp.float32),
            pltpu.VMEM((depth * 8, band), jnp.float32),
            pltpu.SemaphoreType.DMA((len(pieces),)),
        ],
        compiler_params=pltpu.CompilerParams(vmem_limit_bytes=32 * 2**20),
        cost_estimate=pl.CostEstimate(
            flops=2 * rows * held * width, bytes_accessed=2 * held * width, transcendentals=0
        ),
        name="weigh",
    )(weight, *pieces, before)


def body(conductivity, prev_fields, electrodes, data_weight):
    local, depth, cells = prev_fields.shape
    count = lax.axis_size("src")
    band = cells // count
    sources = data_weight.shape[0]
    per = local // UNIT
    slab = lax.axis_index("cells")
    halos = []
    for k in range(per):
        chunk = prev_fields[k * UNIT : (k + 1) * UNIT]
        up = jnp.swapaxes(chunk[:, depth - LOW :], 0, 1)
        down = jnp.swapaxes(chunk[:, :HIGH], 0, 1)
        halos.append(
            (
                lax.ppermute(up, "cells", neighbours("cells", 1)),
                lax.ppermute(down, "cells", neighbours("cells", -1)),
            )
        )
    coefs = stencil_coefficients(conductivity, slab * depth, depth * lax.axis_size("cells"))
    place = jnp.stack([lax.axis_index("src"), slab * (depth * cells)]).astype(jnp.int32)
    weight = fold(place, data_weight, count, per)
    potentials = None
    pieces = []
    for k in range(per):
        low, high = halos[k]
        potentials, kept, *sent = sweep(
            place, prev_fields, low, high, coefs, electrodes, potentials, k * UNIT, UNIT, count, band
        )
        pieces.append(kept)
        for r in range(1, count):
            pairs = [(i, (i + r) % count) for i in range(count)]
            pieces.append(lax.ppermute(sent[r - 1], "src", pairs))
    partial = jnp.zeros((depth * 8, band), jnp.float32)
    done = 0
    for stop in sorted({max(per - 1, 1), per}):
        rows = (stop - done) * UNIT * count
        last = stop == per
        partial = weigh(
            weight,
            pieces[: stop * count],
            partial,
            done * UNIT * count,
            rows,
            depth,
            band,
            1.0 / sources if last else None,
        )
        done = stop
    return (potentials, partial)


def solution(mesh):
    placed = (P("cells", None), P("src", "cells", None), P("src", None), P())
    return jax.shard_map(
        body,
        mesh=mesh,
        in_specs=placed,
        out_specs=(P("src", "cells", None), P("cells", "src")),
        check_vma=False,
    )
```

```python
import functools

import jax
import jax.numpy as jnp
from jax import lax
from jax.experimental import pallas as pl
from jax.experimental.pallas import tpu as pltpu
from jax.sharding import PartitionSpec as P


NY = 32
current = 4.0
LANES = 128
GROUP = 16
ROWS = 32
UNIT = 128
LOW = 2
HIGH = 3


def neighbours(axis, step):
    count = lax.axis_size(axis)
    return [(i, i + step) for i in range(count) if 0 <= i + step < count]


def shift_last(values, offset):
    if offset > 0:
        padding = jnp.zeros(values.shape[:-1] + (offset,), values.dtype)
        return jnp.concatenate([values[..., offset:], padding], axis=-1)
    padding = jnp.zeros(values.shape[:-1] + (-offset,), values.dtype)
    return jnp.concatenate([padding, values[..., :offset]], axis=-1)


def split(values):
    parts = []
    for _ in range(3):
        parts.append(lax.reduce_precision(values, 8, 7))
        values = values - parts[-1]
    rows = jnp.stack(parts, axis=1).astype(jnp.bfloat16)
    return jnp.pad(rows, ((0, 0), (0, GROUP - 3), (0, 0)))


def joined(rows):
    rows = rows[:, :3].astype(jnp.float32)
    return (rows[:, 2] + rows[:, 1]) + rows[:, 0]


def stencil_coefficients(conductivity, low, high, first_plane, planes_total):
    _, cells = conductivity.shape
    padded = jnp.concatenate([low, conductivity, high], axis=0)
    sigma = padded[1:-1]
    column = jnp.arange(cells, dtype=jnp.int32)
    upper = (column % NY != NY - 1).astype(jnp.float32)
    lower = (column % NY != 0).astype(jnp.float32)
    plane = first_plane - 1 + jnp.arange(sigma.shape[0], dtype=jnp.int32)
    inside = ((plane >= 0) & (plane < planes_total))[:, None]
    z_plus = 0.5 * (sigma + padded[2:])
    z_minus = 0.5 * (sigma + padded[:-2])
    y_plus = 0.5 * (sigma + shift_last(sigma, 1) * upper)
    y_minus = 0.5 * (sigma + shift_last(sigma, -1) * lower)
    x_plus = 0.5 * (sigma + shift_last(sigma, NY))
    x_minus = 0.5 * (sigma + shift_last(sigma, -NY))
    diagonal = z_plus + z_minus + y_plus + y_minus + x_plus + x_minus
    scale = jnp.where(inside, 2.0 / jnp.where(inside, diagonal, 1.0), 0.0)
    rows = [
        z_plus * scale,
        z_minus * scale,
        y_plus * scale * upper,
        y_minus * scale * lower,
        x_plus * scale * (column < cells - NY),
        x_minus * scale * (column >= NY),
        current * scale,
        -current * scale,
    ]
    return jnp.stack(rows, axis=1)


def lane_index(shape):
    return lax.broadcasted_iota(jnp.int32, shape, 1)


def sweep_kernel(depth, count, band, place_ref, own_ref, low_ref, high_ref, coef_ref, elec_ref, *refs):
    refs = refs[-(count + 6) :]
    pot_ref, outs, (first, second, extra, final) = refs[0], refs[1 : count + 1], refs[count + 1 : count + 5]
    elec_b = refs[count + 5]
    rows, _, cells = own_ref.shape
    tiles = cells // LANES
    first[0:LOW] = low_ref[...]
    first[LOW : LOW + depth] = jnp.swapaxes(own_ref[...].astype(jnp.float32), 0, 1).astype(jnp.bfloat16)
    first[LOW + depth :] = high_ref[...]
    elec_b[0] = jnp.broadcast_to(elec_ref[:, 0:1], (rows, LANES))
    elec_b[1] = jnp.broadcast_to(elec_ref[:, 1:2], (rows, LANES))
    lane = lane_index((GROUP, LANES))
    left = lane < LANES - NY
    right = lane >= NY
    groups = rows // GROUP

    def spread(row):
        return jnp.broadcast_to(row, (GROUP, LANES))

    def stencil(source, plane, coef_plane, at):
        centre = [source[plane, at, pl.ds(v * LANES, LANES)].astype(jnp.float32) for v in range(tiles)]
        ahead = [pltpu.roll(c, LANES - NY, 1) for c in centre]
        behind = [pltpu.roll(c, NY, 1) for c in centre]

        def tile(v):
            lanes = pl.ds(v * LANES, LANES)

            def coef(kind):
                return spread(coef_ref[coef_plane, kind : kind + 1, lanes])

            x_plus = ahead[v] if v == tiles - 1 else jnp.where(left, ahead[v], ahead[v + 1])
            x_minus = behind[v] if v == 0 else jnp.where(right, behind[v], behind[v - 1])
            total = centre[v] + coef(0) * source[plane + 1, at, lanes].astype(jnp.float32)
            side = coef(1) * source[plane - 1, at, lanes].astype(jnp.float32)
            total = total + coef(2) * pltpu.roll(centre[v], LANES - 1, 1)
            side = side + coef(3) * pltpu.roll(centre[v], 1, 1)
            total = total + coef(4) * x_plus
            side = side + coef(5) * x_minus
            return total + side

        return tile

    def relax_first(plane, at):
        sums = stencil(first, plane + 1, plane, at)
        base = place_ref[1] + (plane - 1) * cells
        plus = elec_b[0, at, :] - base
        minus = elec_b[1, at, :] - base

        def tile(v):
            lanes = pl.ds(v * LANES, LANES)
            strength = spread(coef_ref[plane, 6:7, lanes])
            negative = spread(coef_ref[plane, 7:8, lanes])
            here = lane + v * LANES
            added = jnp.where(plus == here, strength, jnp.where(minus == here, negative, 0.0))
            extra[plane, at, lanes] = added
            second[plane, at, lanes] = sums(v) + added

        return tile

    def relax_second(plane, at):
        sums = stencil(second, plane + 1, plane + 1, at)

        def tile(v):
            lanes = pl.ds(v * LANES, LANES)
            value = sums(v) * (1.0 / 9.0) + extra[plane + 1, at, lanes] * (1.0 / 3.0)
            final[plane, at, lanes] = value.astype(jnp.bfloat16)

        return tile

    spans = [pl.ds(group * GROUP, GROUP) for group in range(groups)]

    def run(makers):
        works = [make() for make in makers]
        for v in range(tiles):
            for work in works:
                work(v)

    def only_first(plane, carry):
        for at in spans:
            run([lambda: relax_first(plane, at)])
        return carry

    def both(plane, carry):
        for at in spans:
            run([lambda: relax_second(plane - 3, at), lambda: relax_first(plane, at)])
        return carry

    lax.fori_loop(0, 3, only_first, 0)
    lax.fori_loop(3, depth + HIGH, both, 0)
    for plane in range(depth + HIGH - 3, depth + 1):
        for at in spans:
            run([lambda: relax_second(plane, at)])
    pot_ref[...] = jnp.swapaxes(final[0:depth].astype(jnp.float32), 0, 1).astype(jnp.bfloat16)

    wide = lane_index((rows, LANES))
    for r in range(count):
        out = outs[r]
        target = lax.rem(place_ref[0] + r, count)
        start = pl.multiple_of(target * band, LANES)
        for plane in range(depth + 1):
            out[:, plane * band : (plane + 1) * band] = final[plane, :, pl.ds(start, band)]
        after = jnp.minimum(target + 1, count - 1)
        after_start = pl.multiple_of(after * band, LANES)
        kept = (target < count - 1).astype(jnp.float32)
        for piece in range(beside_width(depth) // LANES):
            packed = jnp.zeros((rows, LANES), jnp.float32)
            for slot in range(LANES // NY):
                plane = piece * (LANES // NY) + slot
                if plane < depth:
                    row = final[plane, :, pl.ds(after_start, LANES)].astype(jnp.float32)
                    row = pltpu.roll(row, slot * NY, 1) if slot else row
                    mine = (wide >= slot * NY) & (wide < (slot + 1) * NY)
                    packed = jnp.where(mine, row, packed)
            begin = (depth + 1) * band + piece * LANES
            out[:, begin : begin + LANES] = (packed * kept).astype(jnp.bfloat16)


def beside_width(depth):
    return -(-depth * NY // LANES) * LANES


def sweep(place, own, low, high, coefs, electrodes, before, begin, size, count, band):
    _, depth, cells = own.shape
    width = (depth + 1) * band + beside_width(depth)
    block = begin // ROWS
    in_specs = [
        pl.BlockSpec((ROWS, depth, cells), lambda i, place: (i + block, 0, 0)),
        pl.BlockSpec((LOW, ROWS, cells), lambda i, place: (0, i, 0)),
        pl.BlockSpec((HIGH, ROWS, cells), lambda i, place: (0, i, 0)),
        pl.BlockSpec(coefs.shape, lambda i, place: (0, 0, 0)),
        pl.BlockSpec((ROWS, 2), lambda i, place: (i + block, 0)),
    ]
    args = [place, own, low, high, coefs, electrodes]
    aliases = {}
    if before is not None:
        in_specs.append(pl.BlockSpec(memory_space=pl.ANY))
        args.append(before)
        aliases = {6: 0}
    planes = depth + HIGH
    flops = size * cells * planes * 40
    return pl.pallas_call(
        functools.partial(sweep_kernel, depth, count, band),
        grid_spec=pltpu.PrefetchScalarGridSpec(
            num_scalar_prefetch=1,
            grid=(size // ROWS,),
            in_specs=in_specs,
            out_specs=[pl.BlockSpec((ROWS, depth, cells), lambda i, place: (i + block, 0, 0))]
            + [pl.BlockSpec((ROWS, width), lambda i, place: (i, 0))] * count,
            scratch_shapes=[
                pltpu.VMEM((LOW + depth + HIGH, ROWS, cells), jnp.bfloat16),
                pltpu.VMEM((planes, ROWS, cells), jnp.float32),
                pltpu.VMEM((planes, ROWS, cells), jnp.float32),
                pltpu.VMEM((depth + 1, ROWS, cells), jnp.bfloat16),
                pltpu.VMEM((2, ROWS, LANES), jnp.int32),
            ],
        ),
        out_shape=[jax.ShapeDtypeStruct(own.shape, jnp.bfloat16)]
        + [jax.ShapeDtypeStruct((size, width), jnp.bfloat16)] * count,
        input_output_aliases=aliases,
        compiler_params=pltpu.CompilerParams(vmem_limit_bytes=24 * 2**20),
        cost_estimate=pl.CostEstimate(
            flops=flops, bytes_accessed=size * cells * 2 * (3 * depth + LOW + HIGH), transcendentals=0
        ),
        name="sweep",
    )(*args)


def fold_kernel(count, per, place_ref, weight_ref, out_ref):
    total = count * per

    def where_is(block):
        holder = lax.rem(place_ref[0] + count - lax.rem(block, count), count)
        return pl.multiple_of((holder * per + lax.div(block, count)) * UNIT, UNIT)

    for q in range(total):
        here = where_is(q)
        chunk = q // count
        rows = pl.ds(q * UNIT, UNIT)

        def folded(other, carry):
            there = where_is(other)
            straight = weight_ref[pl.ds(here, UNIT), pl.ds(there, UNIT)].astype(jnp.float32)
            turned = weight_ref[pl.ds(there, UNIT), pl.ds(here, UNIT)].astype(jnp.float32)
            columns = pl.ds(pl.multiple_of(other * UNIT, UNIT), UNIT)
            out_ref[rows, columns] = (straight + turned.T).astype(jnp.bfloat16)
            return carry

        if chunk:
            lax.fori_loop(0, chunk * count, folded, 0)
        for other in range(chunk * count, (chunk + 1) * count):
            there = where_is(other)
            out_ref[rows, other * UNIT : (other + 1) * UNIT] = weight_ref[
                pl.ds(here, UNIT), pl.ds(there, UNIT)
            ]
        if chunk + 1 < per:
            out_ref[rows, (chunk + 1) * count * UNIT :] = jnp.zeros(
                (UNIT, (per - chunk - 1) * count * UNIT), jnp.bfloat16
            )


def fold(place, weight, count, per):
    return pl.pallas_call(
        functools.partial(fold_kernel, count, per),
        grid_spec=pltpu.PrefetchScalarGridSpec(
            num_scalar_prefetch=1,
            grid=(1,),
            in_specs=[pl.BlockSpec(weight.shape, lambda i, place: (0, 0))],
            out_specs=pl.BlockSpec(weight.shape, lambda i, place: (0, 0)),
        ),
        out_shape=jax.ShapeDtypeStruct(weight.shape, jnp.bfloat16),
        compiler_params=pltpu.CompilerParams(vmem_limit_bytes=24 * 2**20),
        cost_estimate=pl.CostEstimate(
            flops=weight.size, bytes_accessed=weight.size * 4, transcendentals=0
        ),
        name="fold",
    )(place, weight)


def weigh_kernel(depth, band, pieces, row_start, block_rows, chunk_rows, scale, weight_ref, *refs):
    piece_refs = refs[:pieces]
    before_ref, out_ref, held, mixed, partial, sems = refs[pieces:]
    step = pl.program_id(0)
    tiles = band // LANES

    @pl.when(step == 0)
    def _():
        at = 0
        copies = []
        for i, piece in enumerate(piece_refs):
            size = piece.shape[0]
            copies.append(pltpu.make_async_copy(piece, held.at[pl.ds(at, size)], sems.at[i]))
            copies[-1].start()
            at += size
        for copy in copies:
            copy.wait()
        partial[...] = before_ref[...]

    chunk = (row_start + step * block_rows) // chunk_rows
    for c in range(row_start // chunk_rows, held.shape[0] // chunk_rows):
        reach = (c + 1) * chunk_rows

        @pl.when(chunk == c)
        def _():
            mixed[...] = jnp.dot(
                weight_ref[:, :reach], held[:reach], preferred_element_type=jnp.float32
            )

    lane = lane_index((GROUP, LANES))
    left = lane < LANES - NY
    inner = jnp.where(lax.rem(lane, NY) != NY - 1, 1.0, 0.0)
    base = row_start + step * block_rows

    for plane in range(depth):
        beside_tile = (depth + 1) * band + (plane * NY // LANES) * LANES
        turn = (LANES - NY - plane * NY) % LANES

        def rows_of(group, totals):
            at = pl.ds(pl.multiple_of(group * GROUP, GROUP), GROUP)
            at_held = pl.ds(pl.multiple_of(base + group * GROUP, GROUP), GROUP)

            def read(column):
                lanes = pl.ds(column, LANES)
                return held[at_held, lanes].astype(jnp.float32), mixed[at, lanes]

            centre = [read(plane * band + t * LANES) for t in range(tiles)]
            above = [read((plane + 1) * band + t * LANES) for t in range(tiles)]
            ahead = [tuple(pltpu.roll(c, LANES - NY, 1) for c in pair) for pair in centre]
            ahead.append(tuple(pltpu.roll(c, turn, 1) if turn else c for c in read(beside_tile)))
            result = []
            for t in range(tiles):
                value, product = centre[t]
                total = (above[t][0] - value) * (above[t][1] - product)
                total = total + (jnp.where(left, ahead[t][0], ahead[t + 1][0]) - value) * (
                    jnp.where(left, ahead[t][1], ahead[t + 1][1]) - product
                )
                total = total + (pltpu.roll(value, LANES - 1, 1) * inner - value) * (
                    pltpu.roll(product, LANES - 1, 1) * inner - product
                )
                result.append(totals[t] + (total[:8] + total[8:]))
            return tuple(result)

        rows = pl.ds(plane * 8, 8)
        start = tuple(partial[rows, t * LANES : (t + 1) * LANES] for t in range(tiles))
        sums = lax.fori_loop(0, block_rows // GROUP, rows_of, start, unroll=4)
        for t in range(tiles):
            partial[rows, t * LANES : (t + 1) * LANES] = sums[t]

    @pl.when(step == pl.num_programs(0) - 1)
    def _():
        if scale is None:
            out_ref[...] = partial[...]
        else:
            for plane in range(depth):
                total = jnp.sum(partial[plane * 8 : plane * 8 + 8, :], axis=0, keepdims=True)
                out_ref[plane : plane + 1, :] = total * scale


def weigh(weight, pieces, before, row_start, rows, chunk_rows, depth, band, scale):
    width = pieces[0].shape[1]
    held = sum(piece.shape[0] for piece in pieces)
    block_rows = UNIT
    first = row_start // block_rows
    out = (depth, band) if scale is not None else (depth * 8, band)
    return pl.pallas_call(
        functools.partial(
            weigh_kernel, depth, band, len(pieces), row_start, block_rows, chunk_rows, scale
        ),
        grid=(rows // block_rows,),
        in_specs=[pl.BlockSpec((block_rows, weight.shape[1]), lambda i: (i + first, 0))]
        + [pl.BlockSpec(memory_space=pl.ANY)] * len(pieces)
        + [pl.BlockSpec((depth * 8, band), lambda i: (0, 0))],
        out_specs=pl.BlockSpec(out, lambda i: (0, 0)),
        out_shape=jax.ShapeDtypeStruct(out, jnp.float32),
        scratch_shapes=[
            pltpu.VMEM((held, width), jnp.bfloat16),
            pltpu.VMEM((block_rows, width), jnp.float32),
            pltpu.VMEM((depth * 8, band), jnp.float32),
            pltpu.SemaphoreType.DMA((len(pieces),)),
        ],
        compiler_params=pltpu.CompilerParams(vmem_limit_bytes=32 * 2**20),
        cost_estimate=pl.CostEstimate(
            flops=2 * rows * held * width, bytes_accessed=2 * held * width, transcendentals=0
        ),
        name="weigh",
    )(weight, *pieces, before)


def body(conductivity, prev_fields, electrodes, data_weight):
    local, depth, cells = prev_fields.shape
    count = lax.axis_size("src")
    band = cells // count
    sources = data_weight.shape[0]
    per = local // UNIT
    slab = lax.axis_index("cells")
    halos = []
    fields = prev_fields
    for k in range(per):
        chunk = fields[k * UNIT : (k + 1) * UNIT]
        up = jnp.swapaxes(chunk[:, depth - LOW :], 0, 1)
        down = jnp.swapaxes(chunk[:, :HIGH], 0, 1)
        if k == 0:
            up = jnp.concatenate([up, split(conductivity[depth - LOW :])], axis=1)
            down = jnp.concatenate([down, split(conductivity[:HIGH])], axis=1)
        fields, up, down = lax.optimization_barrier((fields, up, down))
        low = lax.ppermute(up, "cells", neighbours("cells", 1))
        high = lax.ppermute(down, "cells", neighbours("cells", -1))
        halos.append((low, high))
    low, high = (joined(halo[:, UNIT:]) for halo in halos[0])
    coefs = stencil_coefficients(conductivity, low, high, slab * depth, depth * lax.axis_size("cells"))
    place = jnp.stack([lax.axis_index("src"), slab * (depth * cells)]).astype(jnp.int32)
    weight = fold(place, data_weight, count, per)
    potentials = None
    pieces = []
    for k in range(per):
        low, high = halos[k]
        potentials, kept, *sent = sweep(
            place, prev_fields, low, high, coefs, electrodes, potentials, k * UNIT, UNIT, count, band
        )
        pieces.append(kept)
        for r in range(1, count):
            pairs = [(i, (i + r) % count) for i in range(count)]
            pieces.append(lax.ppermute(sent[r - 1], "src", pairs))
    partial = jnp.zeros((depth * 8, band), jnp.float32)
    done = 0
    for stop in sorted({max(per - 1, 1), per}):
        rows = (stop - done) * UNIT * count
        last = stop == per
        partial = weigh(
            weight,
            pieces[: stop * count],
            partial,
            done * UNIT * count,
            rows,
            UNIT * count,
            depth,
            band,
            1.0 / sources if last else None,
        )
        done = stop
    return (potentials, partial)


def solution(mesh):
    placed = (P("cells", None), P("src", "cells", None), P("src", None), P())
    return jax.shard_map(
        body,
        mesh=mesh,
        in_specs=placed,
        out_specs=(P("src", "cells", None), P("cells", "src")),
        check_vma=False,
    )
```

```python
import functools

import jax
import jax.numpy as jnp
from jax import lax
from jax.experimental import pallas as pl
from jax.experimental.pallas import tpu as pltpu
from jax.sharding import PartitionSpec as P


NY = 32
current = 4.0
LANES = 128
GROUP = 16
ROWS = 32
UNIT = 128
HALO = 2
PART = 16


def pairs_of(axis, first):
    count = lax.axis_size(axis)
    pairs = [(i, i + 1) for i in range(first, count - 1, 2)]
    return pairs + [(b, a) for a, b in pairs]


def split(values):
    parts = []
    for _ in range(3):
        parts.append(lax.reduce_precision(values, 8, 7))
        values = values - parts[-1]
    rows = jnp.stack(parts, axis=1).astype(jnp.bfloat16)
    return jnp.pad(rows, ((0, 0), (0, PART - 3), (0, 0)))


def coefficient_kernel(depth, planes_total, place_ref, sigma_ref, inner_ref, outer_ref, out_ref, padded):
    cells = sigma_ref.shape[1]
    planes = depth + 2
    odd = place_ref[2]

    def put(at, ref):
        for i in range(HALO):
            part = ref[i].astype(jnp.float32)
            padded[at + i : at + i + 1, :] = (part[2:3] + part[1:2]) + part[0:1]

    padded[HALO : HALO + depth, :] = sigma_ref[...]

    @pl.when(odd == 0)
    def _():
        put(0, outer_ref)
        put(HALO + depth, inner_ref)

    @pl.when(odd == 1)
    def _():
        put(0, inner_ref)
        put(HALO + depth, outer_ref)

    sigma = padded[1 : planes + 1, :]
    column = lax.broadcasted_iota(jnp.int32, sigma.shape, 1)
    row = lax.rem(column, NY)
    plane = lax.div(place_ref[1], cells) - 1 + lax.broadcasted_iota(jnp.int32, sigma.shape, 0)
    inside = (plane >= 0) & (plane < planes_total)
    zero = jnp.zeros_like(sigma)
    upper, lower = row != NY - 1, row != 0
    ahead, behind = column < cells - NY, column >= NY
    z_plus = 0.5 * (sigma + padded[2 : planes + 2, :])
    z_minus = 0.5 * (sigma + padded[0:planes, :])
    y_plus = 0.5 * (sigma + jnp.where(upper, pltpu.roll(sigma, cells - 1, 1), zero))
    y_minus = 0.5 * (sigma + jnp.where(lower, pltpu.roll(sigma, 1, 1), zero))
    x_plus = 0.5 * (sigma + jnp.where(ahead, pltpu.roll(sigma, cells - NY, 1), zero))
    x_minus = 0.5 * (sigma + jnp.where(behind, pltpu.roll(sigma, NY, 1), zero))
    diagonal = z_plus + z_minus + y_plus + y_minus + x_plus + x_minus
    scale = jnp.where(inside, 2.0 / jnp.where(inside, diagonal, 1.0), zero)
    kinds = [
        z_plus * scale,
        z_minus * scale,
        jnp.where(upper, y_plus * scale, zero),
        jnp.where(lower, y_minus * scale, zero),
        jnp.where(ahead, x_plus * scale, zero),
        jnp.where(behind, x_minus * scale, zero),
        current * scale,
        -current * scale,
    ]
    for kind, values in enumerate(kinds):
        for i in range(planes):
            out_ref[i, kind : kind + 1, :] = values[i : i + 1, :]


def stencil_coefficients(place, conductivity, inner, outer, planes_total):
    depth, cells = conductivity.shape
    part = inner.shape[1] // PART - 1
    shape = (depth + 2, 8, cells)
    return pl.pallas_call(
        functools.partial(coefficient_kernel, depth, planes_total),
        grid_spec=pltpu.PrefetchScalarGridSpec(
            num_scalar_prefetch=1,
            grid=(1,),
            in_specs=[pl.BlockSpec((depth, cells), lambda i, place: (0, 0))]
            + [pl.BlockSpec((HALO, PART, cells), lambda i, place: (0, part, 0))] * 2,
            out_specs=pl.BlockSpec(shape, lambda i, place: (0, 0, 0)),
            scratch_shapes=[pltpu.VMEM((2 * HALO + depth, cells), jnp.float32)],
        ),
        out_shape=jax.ShapeDtypeStruct(shape, jnp.float32),
        compiler_params=pltpu.CompilerParams(vmem_limit_bytes=8 * 2**20),
        name="coefficients",
    )(place, conductivity, inner, outer)


def lane_index(shape):
    return lax.broadcasted_iota(jnp.int32, shape, 1)


def sweep_kernel(depth, count, band, place_ref, own_ref, inner_ref, outer_ref, coef_ref, elec_ref, *refs):
    refs = refs[-(count + 6) :]
    pot_ref, outs, (first, second, extra, final) = refs[0], refs[1 : count + 1], refs[count + 1 : count + 5]
    elec_b = refs[count + 5]
    _, rows, cells = own_ref.shape
    tiles = cells // LANES
    first[HALO : HALO + depth] = own_ref[...]

    @pl.when(place_ref[2] == 0)
    def _():
        first[0:HALO] = outer_ref[...]
        first[HALO + depth :] = inner_ref[...]

    @pl.when(place_ref[2] == 1)
    def _():
        first[0:HALO] = inner_ref[...]
        first[HALO + depth :] = outer_ref[...]

    elec_b[0] = jnp.broadcast_to(elec_ref[:, 0:1], (rows, LANES))
    elec_b[1] = jnp.broadcast_to(elec_ref[:, 1:2], (rows, LANES))
    lane = lane_index((GROUP, LANES))
    left = lane < LANES - NY
    right = lane >= NY
    groups = rows // GROUP

    def spread(row):
        return jnp.broadcast_to(row, (GROUP, LANES))

    def stencil(source, plane, coef_plane, at):
        centre = [source[plane, at, pl.ds(v * LANES, LANES)].astype(jnp.float32) for v in range(tiles)]
        ahead = [pltpu.roll(c, LANES - NY, 1) for c in centre]
        behind = [pltpu.roll(c, NY, 1) for c in centre]

        def tile(v):
            lanes = pl.ds(v * LANES, LANES)

            def coef(kind):
                return spread(coef_ref[coef_plane, kind : kind + 1, lanes])

            x_plus = ahead[v] if v == tiles - 1 else jnp.where(left, ahead[v], ahead[v + 1])
            x_minus = behind[v] if v == 0 else jnp.where(right, behind[v], behind[v - 1])
            total = centre[v] + coef(0) * source[plane + 1, at, lanes].astype(jnp.float32)
            side = coef(1) * source[plane - 1, at, lanes].astype(jnp.float32)
            total = total + coef(2) * pltpu.roll(centre[v], LANES - 1, 1)
            side = side + coef(3) * pltpu.roll(centre[v], 1, 1)
            total = total + coef(4) * x_plus
            side = side + coef(5) * x_minus
            return total + side

        return tile

    def relax_first(plane, at):
        sums = stencil(first, plane + 1, plane, at)
        base = place_ref[1] + (plane - 1) * cells
        plus = elec_b[0, at, :] - base
        minus = elec_b[1, at, :] - base

        def tile(v):
            lanes = pl.ds(v * LANES, LANES)
            strength = spread(coef_ref[plane, 6:7, lanes])
            negative = spread(coef_ref[plane, 7:8, lanes])
            here = lane + v * LANES
            added = jnp.where(plus == here, strength, jnp.where(minus == here, negative, 0.0))
            extra[plane, at, lanes] = added
            second[plane, at, lanes] = sums(v) + added

        return tile

    def relax_second(plane, at):
        sums = stencil(second, plane + 1, plane + 1, at)

        def tile(v):
            lanes = pl.ds(v * LANES, LANES)
            value = sums(v) * (1.0 / 9.0) + extra[plane + 1, at, lanes] * (1.0 / 3.0)
            final[plane, at, lanes] = value.astype(jnp.bfloat16)

        return tile

    spans = [pl.ds(group * GROUP, GROUP) for group in range(groups)]

    def run(makers):
        works = [make() for make in makers]
        for v in range(tiles):
            for work in works:
                work(v)

    def only_first(plane, carry):
        for at in spans:
            run([lambda: relax_first(plane, at)])
        return carry

    def both(plane, carry):
        for at in spans:
            run([lambda: relax_second(plane - 3, at), lambda: relax_first(plane, at)])
        return carry

    planes = depth + 2
    lax.fori_loop(0, 3, only_first, 0)
    lax.fori_loop(3, planes, both, 0)
    for plane in range(planes - 3, depth):
        for at in spans:
            run([lambda: relax_second(plane, at)])
    pot_ref[...] = final[...]

    wide = lane_index((rows, LANES))
    for r in range(count):
        out = outs[r]
        target = lax.rem(place_ref[0] + r, count)
        start = pl.multiple_of(target * band, LANES)
        for plane in range(depth):
            out[:, plane * band : (plane + 1) * band] = final[plane, :, pl.ds(start, band)]
        after = jnp.minimum(target + 1, count - 1)
        after_start = pl.multiple_of(after * band, LANES)
        kept = (target < count - 1).astype(jnp.float32)
        for piece in range(beside_width(depth) // LANES):
            packed = jnp.zeros((rows, LANES), jnp.float32)
            for slot in range(LANES // NY):
                plane = piece * (LANES // NY) + slot
                if plane < depth:
                    row = final[plane, :, pl.ds(after_start, LANES)].astype(jnp.float32)
                    row = pltpu.roll(row, slot * NY, 1) if slot else row
                    mine = (wide >= slot * NY) & (wide < (slot + 1) * NY)
                    packed = jnp.where(mine, row, packed)
            begin = depth * band + piece * LANES
            out[:, begin : begin + LANES] = (packed * kept).astype(jnp.bfloat16)


def beside_width(depth):
    return -(-depth * NY // LANES) * LANES


def sweep(place, own, inner, outer, coefs, electrodes, before, begin, size, count, band):
    depth, _, cells = own.shape
    width = depth * band + beside_width(depth)
    block = begin // ROWS
    in_specs = [
        pl.BlockSpec((depth, ROWS, cells), lambda i, place: (0, i + block, 0)),
        pl.BlockSpec((HALO, ROWS, cells), lambda i, place: (0, i, 0)),
        pl.BlockSpec((HALO, ROWS, cells), lambda i, place: (0, i, 0)),
        pl.BlockSpec(coefs.shape, lambda i, place: (0, 0, 0)),
        pl.BlockSpec((ROWS, 2), lambda i, place: (i + block, 0)),
    ]
    args = [place, own, inner, outer, coefs, electrodes]
    aliases = {}
    if before is not None:
        in_specs.append(pl.BlockSpec(memory_space=pl.ANY))
        args.append(before)
        aliases = {6: 0}
    planes = depth + 2
    flops = size * cells * planes * 40
    return pl.pallas_call(
        functools.partial(sweep_kernel, depth, count, band),
        grid_spec=pltpu.PrefetchScalarGridSpec(
            num_scalar_prefetch=1,
            grid=(size // ROWS,),
            in_specs=in_specs,
            out_specs=[pl.BlockSpec((depth, ROWS, cells), lambda i, place: (0, i + block, 0))]
            + [pl.BlockSpec((ROWS, width), lambda i, place: (i, 0))] * count,
            scratch_shapes=[
                pltpu.VMEM((2 * HALO + depth, ROWS, cells), jnp.bfloat16),
                pltpu.VMEM((planes, ROWS, cells), jnp.float32),
                pltpu.VMEM((planes, ROWS, cells), jnp.float32),
                pltpu.VMEM((depth, ROWS, cells), jnp.bfloat16),
                pltpu.VMEM((2, ROWS, LANES), jnp.int32),
            ],
        ),
        out_shape=[jax.ShapeDtypeStruct(own.shape, jnp.bfloat16)]
        + [jax.ShapeDtypeStruct((size, width), jnp.bfloat16)] * count,
        input_output_aliases=aliases,
        compiler_params=pltpu.CompilerParams(vmem_limit_bytes=24 * 2**20),
        cost_estimate=pl.CostEstimate(
            flops=flops, bytes_accessed=size * cells * 2 * (3 * depth + 2 * HALO), transcendentals=0
        ),
        name="sweep",
    )(*args)


def fold_kernel(count, per, place_ref, weight_ref, out_ref):
    total = count * per

    def where_is(block):
        holder = lax.rem(place_ref[0] + count - lax.rem(block, count), count)
        return pl.multiple_of((holder * per + lax.div(block, count)) * UNIT, UNIT)

    for q in range(total):
        here = where_is(q)
        chunk = q // count
        rows = pl.ds(q * UNIT, UNIT)

        def folded(other, carry):
            there = where_is(other)
            straight = weight_ref[pl.ds(here, UNIT), pl.ds(there, UNIT)].astype(jnp.float32)
            turned = weight_ref[pl.ds(there, UNIT), pl.ds(here, UNIT)].astype(jnp.float32)
            columns = pl.ds(pl.multiple_of(other * UNIT, UNIT), UNIT)
            out_ref[rows, columns] = (straight + turned.T).astype(jnp.bfloat16)
            return carry

        if chunk:
            lax.fori_loop(0, chunk * count, folded, 0)
        for other in range(chunk * count, (chunk + 1) * count):
            there = where_is(other)
            out_ref[rows, other * UNIT : (other + 1) * UNIT] = weight_ref[
                pl.ds(here, UNIT), pl.ds(there, UNIT)
            ]
        if chunk + 1 < per:
            out_ref[rows, (chunk + 1) * count * UNIT :] = jnp.zeros(
                (UNIT, (per - chunk - 1) * count * UNIT), jnp.bfloat16
            )


def fold(place, weight, count, per):
    return pl.pallas_call(
        functools.partial(fold_kernel, count, per),
        grid_spec=pltpu.PrefetchScalarGridSpec(
            num_scalar_prefetch=1,
            grid=(1,),
            in_specs=[pl.BlockSpec(weight.shape, lambda i, place: (0, 0))],
            out_specs=pl.BlockSpec(weight.shape, lambda i, place: (0, 0)),
        ),
        out_shape=jax.ShapeDtypeStruct(weight.shape, jnp.bfloat16),
        compiler_params=pltpu.CompilerParams(vmem_limit_bytes=24 * 2**20),
        cost_estimate=pl.CostEstimate(
            flops=weight.size, bytes_accessed=weight.size * 4, transcendentals=0
        ),
        name="fold",
    )(place, weight)


def weigh_kernel(depth, band, pieces, above, row_start, block_rows, chunk_rows, scale, weight_ref, *refs):
    piece_refs, above_refs = refs[:pieces], refs[pieces : pieces + above]
    before_ref, out_ref, held, mixed, partial, sems = refs[pieces + above :]
    step = pl.program_id(0)
    tiles = band // LANES
    wide = depth * band + beside_width(depth)

    @pl.when(step == 0)
    def _():
        copies = []
        for group, column in ((piece_refs, 0), (above_refs, wide)):
            at = 0
            for ref in group:
                size, width = ref.shape
                into = held.at[pl.ds(at, size), pl.ds(column, width)]
                copies.append(pltpu.make_async_copy(ref, into, sems.at[len(copies)]))
                copies[-1].start()
                at += size
        for copy in copies:
            copy.wait()
        partial[...] = before_ref[...]

    chunk = (row_start + step * block_rows) // chunk_rows
    for c in range(row_start // chunk_rows, held.shape[0] // chunk_rows):
        reach = (c + 1) * chunk_rows

        @pl.when(chunk == c)
        def _():
            mixed[...] = jnp.dot(
                weight_ref[:, :reach], held[:reach], preferred_element_type=jnp.float32
            )

    lane = lane_index((GROUP, LANES))
    left = lane < LANES - NY
    inner = jnp.where(lax.rem(lane, NY) != NY - 1, 1.0, 0.0)
    base = row_start + step * block_rows

    for plane in range(depth):
        beside_tile = depth * band + (plane * NY // LANES) * LANES
        turn = (LANES - NY - plane * NY) % LANES

        def rows_of(group, totals):
            at = pl.ds(pl.multiple_of(group * GROUP, GROUP), GROUP)
            at_held = pl.ds(pl.multiple_of(base + group * GROUP, GROUP), GROUP)

            def read(column):
                lanes = pl.ds(column, LANES)
                return held[at_held, lanes].astype(jnp.float32), mixed[at, lanes]

            centre = [read(plane * band + t * LANES) for t in range(tiles)]
            over = (plane + 1) * band if plane < depth - 1 else wide
            above = [read(over + t * LANES) for t in range(tiles)]
            ahead = [tuple(pltpu.roll(c, LANES - NY, 1) for c in pair) for pair in centre]
            ahead.append(tuple(pltpu.roll(c, turn, 1) if turn else c for c in read(beside_tile)))
            result = []
            for t in range(tiles):
                value, product = centre[t]
                total = (above[t][0] - value) * (above[t][1] - product)
                total = total + (jnp.where(left, ahead[t][0], ahead[t + 1][0]) - value) * (
                    jnp.where(left, ahead[t][1], ahead[t + 1][1]) - product
                )
                total = total + (pltpu.roll(value, LANES - 1, 1) * inner - value) * (
                    pltpu.roll(product, LANES - 1, 1) * inner - product
                )
                result.append(totals[t] + (total[:8] + total[8:]))
            return tuple(result)

        rows = pl.ds(plane * 8, 8)
        start = tuple(partial[rows, t * LANES : (t + 1) * LANES] for t in range(tiles))
        sums = lax.fori_loop(0, block_rows // GROUP, rows_of, start, unroll=4)
        for t in range(tiles):
            partial[rows, t * LANES : (t + 1) * LANES] = sums[t]

    @pl.when(step == pl.num_programs(0) - 1)
    def _():
        if scale is None:
            out_ref[...] = partial[...]
        else:
            for plane in range(depth):
                total = jnp.sum(partial[plane * 8 : plane * 8 + 8, :], axis=0, keepdims=True)
                out_ref[plane : plane + 1, :] = total * scale


def weigh(weight, pieces, above, before, row_start, rows, chunk_rows, depth, band, scale):
    width = pieces[0].shape[1] + band
    held = sum(piece.shape[0] for piece in pieces)
    block_rows = UNIT
    first = row_start // block_rows
    out = (depth, band) if scale is not None else (depth * 8, band)
    return pl.pallas_call(
        functools.partial(
            weigh_kernel, depth, band, len(pieces), len(above), row_start, block_rows, chunk_rows, scale
        ),
        grid=(rows // block_rows,),
        in_specs=[pl.BlockSpec((block_rows, weight.shape[1]), lambda i: (i + first, 0))]
        + [pl.BlockSpec(memory_space=pl.ANY)] * (len(pieces) + len(above))
        + [pl.BlockSpec((depth * 8, band), lambda i: (0, 0))],
        out_specs=pl.BlockSpec(out, lambda i: (0, 0)),
        out_shape=jax.ShapeDtypeStruct(out, jnp.float32),
        scratch_shapes=[
            pltpu.VMEM((held, width), jnp.bfloat16),
            pltpu.VMEM((block_rows, width), jnp.float32),
            pltpu.VMEM((depth * 8, band), jnp.float32),
            pltpu.SemaphoreType.DMA((len(pieces) + len(above),)),
        ],
        compiler_params=pltpu.CompilerParams(vmem_limit_bytes=32 * 2**20),
        cost_estimate=pl.CostEstimate(
            flops=2 * rows * held * width, bytes_accessed=2 * held * width, transcendentals=0
        ),
        name="weigh",
    )(weight, *pieces, *above, before)


def body(conductivity, prev_fields, electrodes, data_weight):
    local, depth, cells = prev_fields.shape
    count = lax.axis_size("src")
    band = cells // count
    sources = data_weight.shape[0]
    per = local // UNIT
    slab = lax.axis_index("cells")
    odd = lax.rem(slab, 2)
    place = jnp.stack([lax.axis_index("src"), slab * (depth * cells), odd]).astype(jnp.int32)
    own = jnp.swapaxes(prev_fields, 0, 1)
    bottom, top = jnp.int32(0), jnp.int32(depth - HALO)
    halos = []
    for k in range(per):
        received = []
        for first, start in (
            (0, jnp.where(odd == 0, top, bottom)), (1, jnp.where(odd == 0, bottom, top))
        ):
            planes = lax.dynamic_slice(own, (start, k * UNIT, 0), (HALO, UNIT, cells))
            if k == 0:
                sigma = lax.dynamic_slice_in_dim(conductivity, start, HALO, axis=0)
                planes = jnp.concatenate([planes, split(sigma)], axis=1)
            received.append(lax.ppermute(planes, "cells", pairs_of("cells", first)))
        halos.append(received)
    coefs = stencil_coefficients(place, conductivity, *halos[0], depth * lax.axis_size("cells"))
    weight = fold(place, data_weight, count, per)
    down = [(i + 1, i) for i in range(lax.axis_size("cells") - 1)]
    stops = [stop for stop in (per - 2, per - 1, per) if stop > 0]
    potentials = None
    pieces, above = [], []
    sums = jnp.zeros((depth * 8, band), jnp.float32)
    done = 0
    for k in range(per):
        potentials, kept, *sent = sweep(
            place, own, *halos[k], coefs, electrodes, potentials, k * UNIT, UNIT, count, band
        )
        pieces.append(kept)
        for r in range(1, count):
            pairs = [(i, (i + r) % count) for i in range(count)]
            pieces.append(lax.ppermute(sent[r - 1], "src", pairs))
    for stop in stops:
        lowest = jnp.concatenate([p[:, :band] for p in pieces[done * count : stop * count]], axis=0)
        above.append(lax.ppermute(lowest, "cells", down))
        sums = weigh(
            weight,
            pieces[: stop * count],
            above,
            sums,
            done * UNIT * count,
            (stop - done) * UNIT * count,
            UNIT * count,
            depth,
            band,
            1.0 / sources if stop == per else None,
        )
        done = stop
    return (jnp.swapaxes(potentials, 0, 1), sums)


def solution(mesh):
    placed = (P("cells", None), P("src", "cells", None), P("src", None), P())
    return jax.shard_map(
        body,
        mesh=mesh,
        in_specs=placed,
        out_specs=(P("src", "cells", None), P("cells", "src")),
        check_vma=False,
    )
```

```python
import functools

import jax
import jax.numpy as jnp
from jax import lax
from jax.experimental import pallas as pl
from jax.experimental.pallas import tpu as pltpu
from jax.sharding import PartitionSpec as P


NY = 32
current = 4.0
LANES = 128
GROUP = 16
ROWS = 32
UNIT = 128
HALO = 2
PART = 16


def pairs_of(axis, first):
    count = lax.axis_size(axis)
    pairs = [(i, i + 1) for i in range(first, count - 1, 2)]
    return pairs + [(b, a) for a, b in pairs]


def coefficient_kernel(depth, planes_total, sigma_ref, inner_ref, outer_ref, out_ref, padded):
    cells = sigma_ref.shape[1]
    planes = depth + 2
    slab = lax.axis_index("cells")
    odd = lax.rem(slab, 2)

    def put(at, ref):
        for i in range(HALO):
            part = ref[i].astype(jnp.float32)
            padded[at + i : at + i + 1, :] = (part[2:3] + part[1:2]) + part[0:1]

    padded[HALO : HALO + depth, :] = sigma_ref[...]

    @pl.when(odd == 0)
    def _():
        put(0, outer_ref)
        put(HALO + depth, inner_ref)

    @pl.when(odd == 1)
    def _():
        put(0, inner_ref)
        put(HALO + depth, outer_ref)

    sigma = padded[1 : planes + 1, :]
    column = lax.broadcasted_iota(jnp.int32, sigma.shape, 1)
    row = lax.rem(column, NY)
    plane = slab * depth - 1 + lax.broadcasted_iota(jnp.int32, sigma.shape, 0)
    inside = (plane >= 0) & (plane < planes_total)
    zero = jnp.zeros_like(sigma)
    upper, lower = row != NY - 1, row != 0
    ahead, behind = column < cells - NY, column >= NY
    z_plus = 0.5 * (sigma + padded[2 : planes + 2, :])
    z_minus = 0.5 * (sigma + padded[0:planes, :])
    y_plus = 0.5 * (sigma + jnp.where(upper, pltpu.roll(sigma, cells - 1, 1), zero))
    y_minus = 0.5 * (sigma + jnp.where(lower, pltpu.roll(sigma, 1, 1), zero))
    x_plus = 0.5 * (sigma + jnp.where(ahead, pltpu.roll(sigma, cells - NY, 1), zero))
    x_minus = 0.5 * (sigma + jnp.where(behind, pltpu.roll(sigma, NY, 1), zero))
    diagonal = z_plus + z_minus + y_plus + y_minus + x_plus + x_minus
    scale = jnp.where(inside, 2.0 / jnp.where(inside, diagonal, 1.0), zero)
    kinds = [
        z_plus * scale,
        z_minus * scale,
        jnp.where(upper, y_plus * scale, zero),
        jnp.where(lower, y_minus * scale, zero),
        jnp.where(ahead, x_plus * scale, zero),
        jnp.where(behind, x_minus * scale, zero),
        current * scale,
        -current * scale,
    ]
    for kind, values in enumerate(kinds):
        for i in range(planes):
            out_ref[i, kind : kind + 1, :] = values[i : i + 1, :]


def stencil_coefficients(conductivity, inner, outer, planes_total):
    depth, cells = conductivity.shape
    part = inner.shape[1] // PART - 1
    shape = (depth + 2, 8, cells)
    return pl.pallas_call(
        functools.partial(coefficient_kernel, depth, planes_total),
        grid=(1,),
        in_specs=[pl.BlockSpec((depth, cells), lambda i: (0, 0))]
        + [pl.BlockSpec((HALO, PART, cells), lambda i: (0, part, 0))] * 2,
        out_specs=pl.BlockSpec(shape, lambda i: (0, 0, 0)),
        out_shape=jax.ShapeDtypeStruct(shape, jnp.float32),
        scratch_shapes=[pltpu.VMEM((2 * HALO + depth, cells), jnp.float32)],
        compiler_params=pltpu.CompilerParams(vmem_limit_bytes=8 * 2**20),
        name="coefficients",
    )(conductivity, inner, outer)


def pack_kernel(extra, fields_ref, sigma_ref, own_ref, inner_ref, outer_ref):
    rows, depth, cells = fields_ref.shape
    odd = lax.rem(lax.axis_index("cells"), 2)
    own_ref[...] = jnp.swapaxes(fields_ref[...].astype(jnp.float32), 0, 1).astype(jnp.bfloat16)

    def part(plane):
        rest = jnp.broadcast_to(sigma_ref[plane : plane + 1, :], (PART, cells))
        row = lax.broadcasted_iota(jnp.int32, rest.shape, 0)
        parts = jnp.zeros_like(rest)
        for i in range(3):
            rounded = rest.astype(jnp.bfloat16).astype(jnp.float32)
            parts = jnp.where(row == i, rounded, parts)
            rest = rest - rounded
        return parts.astype(jnp.bfloat16)

    def pick(out_ref, start):
        out_ref[:, 0:rows] = own_ref[start : start + HALO]
        if extra:
            for i in range(HALO):
                out_ref[i, rows : rows + PART, :] = part(start + i)

    @pl.when(odd == 0)
    def _():
        pick(inner_ref, depth - HALO)
        pick(outer_ref, 0)

    @pl.when(odd == 1)
    def _():
        pick(inner_ref, 0)
        pick(outer_ref, depth - HALO)


def pack(fields, conductivity, k):
    _, depth, cells = fields.shape
    extra = k == 0
    rows = UNIT if extra else ROWS
    steps = UNIT // rows
    sent = UNIT + (PART if extra else 0)
    block = sent if extra else rows
    return pl.pallas_call(
        functools.partial(pack_kernel, extra),
        grid=(steps,),
        in_specs=[
            pl.BlockSpec((rows, depth, cells), lambda i: (i + k * steps, 0, 0)),
            pl.BlockSpec((depth, cells), lambda i: (0, 0)),
        ],
        out_specs=[pl.BlockSpec((depth, rows, cells), lambda i: (0, i, 0))]
        + [pl.BlockSpec((HALO, block, cells), lambda i: (0, i, 0))] * 2,
        out_shape=[jax.ShapeDtypeStruct((depth, UNIT, cells), jnp.bfloat16)]
        + [jax.ShapeDtypeStruct((HALO, sent, cells), jnp.bfloat16)] * 2,
        compiler_params=pltpu.CompilerParams(vmem_limit_bytes=60 * 2**20),
        name="pack",
    )(fields, conductivity)


def lane_index(shape):
    return lax.broadcasted_iota(jnp.int32, shape, 1)


def sweep_kernel(count, band, own_ref, inner_ref, outer_ref, coef_ref, elec_ref, *refs):
    refs = refs[-(count + 6) :]
    pot_ref, outs, (first, second, extra, final) = refs[0], refs[1 : count + 1], refs[count + 1 : count + 5]
    elec_b = refs[count + 5]
    depth, rows, cells = own_ref.shape
    slab = lax.axis_index("cells")
    odd = lax.rem(slab, 2)
    tiles = cells // LANES
    first[HALO : HALO + depth] = own_ref[...]

    @pl.when(odd == 0)
    def _():
        first[0:HALO] = outer_ref[...]
        first[HALO + depth :] = inner_ref[...]

    @pl.when(odd == 1)
    def _():
        first[0:HALO] = inner_ref[...]
        first[HALO + depth :] = outer_ref[...]

    elec_b[0] = jnp.broadcast_to(elec_ref[:, 0:1], (rows, LANES))
    elec_b[1] = jnp.broadcast_to(elec_ref[:, 1:2], (rows, LANES))
    lane = lane_index((GROUP, LANES))
    left = lane < LANES - NY
    right = lane >= NY
    groups = rows // GROUP

    def spread(row):
        return jnp.broadcast_to(row, (GROUP, LANES))

    def stencil(source, plane, coef_plane, at):
        centre = [source[plane, at, pl.ds(v * LANES, LANES)].astype(jnp.float32) for v in range(tiles)]
        ahead = [pltpu.roll(c, LANES - NY, 1) for c in centre]
        behind = [pltpu.roll(c, NY, 1) for c in centre]

        def tile(v):
            lanes = pl.ds(v * LANES, LANES)

            def coef(kind):
                return spread(coef_ref[coef_plane, kind : kind + 1, lanes])

            x_plus = ahead[v] if v == tiles - 1 else jnp.where(left, ahead[v], ahead[v + 1])
            x_minus = behind[v] if v == 0 else jnp.where(right, behind[v], behind[v - 1])
            total = centre[v] + coef(0) * source[plane + 1, at, lanes].astype(jnp.float32)
            side = coef(1) * source[plane - 1, at, lanes].astype(jnp.float32)
            total = total + coef(2) * pltpu.roll(centre[v], LANES - 1, 1)
            side = side + coef(3) * pltpu.roll(centre[v], 1, 1)
            total = total + coef(4) * x_plus
            side = side + coef(5) * x_minus
            return total + side

        return tile

    def relax_first(plane, at):
        sums = stencil(first, plane + 1, plane, at)
        base = (slab * depth + plane - 1) * cells
        plus = elec_b[0, at, :] - base
        minus = elec_b[1, at, :] - base

        def tile(v):
            lanes = pl.ds(v * LANES, LANES)
            strength = spread(coef_ref[plane, 6:7, lanes])
            negative = spread(coef_ref[plane, 7:8, lanes])
            here = lane + v * LANES
            added = jnp.where(plus == here, strength, jnp.where(minus == here, negative, 0.0))
            extra[plane, at, lanes] = added
            second[plane, at, lanes] = sums(v) + added

        return tile

    def relax_second(plane, at):
        sums = stencil(second, plane + 1, plane + 1, at)

        def tile(v):
            lanes = pl.ds(v * LANES, LANES)
            value = sums(v) * (1.0 / 9.0) + extra[plane + 1, at, lanes] * (1.0 / 3.0)
            final[plane, at, lanes] = value.astype(jnp.bfloat16)

        return tile

    spans = [pl.ds(group * GROUP, GROUP) for group in range(groups)]

    def run(makers):
        works = [make() for make in makers]
        for v in range(tiles):
            for work in works:
                work(v)

    def only_first(plane, carry):
        for at in spans:
            run([lambda: relax_first(plane, at)])
        return carry

    def both(plane, carry):
        for at in spans:
            run([lambda: relax_second(plane - 3, at), lambda: relax_first(plane, at)])
        return carry

    planes = depth + 2
    lax.fori_loop(0, 3, only_first, 0)
    lax.fori_loop(3, planes, both, 0)
    for plane in range(planes - 3, depth):
        for at in spans:
            run([lambda: relax_second(plane, at)])
    pot_ref[...] = jnp.swapaxes(final[...].astype(jnp.float32), 0, 1).astype(jnp.bfloat16)

    wide = lane_index((rows, LANES))
    for r in range(count):
        out = outs[r]
        target = lax.rem(lax.axis_index("src") + r, count)
        start = pl.multiple_of(target * band, LANES)
        for plane in range(depth):
            out[:, plane * band : (plane + 1) * band] = final[plane, :, pl.ds(start, band)]
        after = jnp.minimum(target + 1, count - 1)
        after_start = pl.multiple_of(after * band, LANES)
        kept = (target < count - 1).astype(jnp.float32)
        for piece in range(beside_width(depth) // LANES):
            packed = jnp.zeros((rows, LANES), jnp.float32)
            for slot in range(LANES // NY):
                plane = piece * (LANES // NY) + slot
                if plane < depth:
                    row = final[plane, :, pl.ds(after_start, LANES)].astype(jnp.float32)
                    row = pltpu.roll(row, slot * NY, 1) if slot else row
                    mine = (wide >= slot * NY) & (wide < (slot + 1) * NY)
                    packed = jnp.where(mine, row, packed)
            begin = depth * band + piece * LANES
            out[:, begin : begin + LANES] = (packed * kept).astype(jnp.bfloat16)


def beside_width(depth):
    return -(-depth * NY // LANES) * LANES


def sweep(own, inner, outer, coefs, electrodes, before, total, begin, count, band):
    depth, size, cells = own.shape
    width = depth * band + beside_width(depth)
    block = begin // ROWS
    in_specs = [
        pl.BlockSpec((depth, ROWS, cells), lambda i: (0, i, 0)),
        pl.BlockSpec((HALO, ROWS, cells), lambda i: (0, i, 0)),
        pl.BlockSpec((HALO, ROWS, cells), lambda i: (0, i, 0)),
        pl.BlockSpec(coefs.shape, lambda i: (0, 0, 0)),
        pl.BlockSpec((ROWS, 2), lambda i: (i + block, 0)),
    ]
    args = [own, inner, outer, coefs, electrodes]
    aliases = {}
    if before is not None:
        in_specs.append(pl.BlockSpec(memory_space=pl.ANY))
        args.append(before)
        aliases = {5: 0}
    planes = depth + 2
    return pl.pallas_call(
        functools.partial(sweep_kernel, count, band),
        grid=(size // ROWS,),
        in_specs=in_specs,
        out_specs=[pl.BlockSpec((ROWS, depth, cells), lambda i: (i + block, 0, 0))]
        + [pl.BlockSpec((ROWS, width), lambda i: (i, 0))] * count,
        scratch_shapes=[
            pltpu.VMEM((2 * HALO + depth, ROWS, cells), jnp.bfloat16),
            pltpu.VMEM((planes, ROWS, cells), jnp.float32),
            pltpu.VMEM((planes, ROWS, cells), jnp.float32),
            pltpu.VMEM((depth, ROWS, cells), jnp.bfloat16),
            pltpu.VMEM((2, ROWS, LANES), jnp.int32),
        ],
        out_shape=[jax.ShapeDtypeStruct((total, depth, cells), jnp.bfloat16)]
        + [jax.ShapeDtypeStruct((size, width), jnp.bfloat16)] * count,
        input_output_aliases=aliases,
        compiler_params=pltpu.CompilerParams(vmem_limit_bytes=44 * 2**20),
        cost_estimate=pl.CostEstimate(
            flops=size * cells * planes * 40,
            bytes_accessed=size * cells * 2 * (3 * depth + 2 * HALO),
            transcendentals=0,
        ),
        name="sweep",
    )(*args)


def fold_kernel(count, per, weight_ref, out_ref):
    total = count * per

    def where_is(block):
        holder = lax.rem(lax.axis_index("src") + count - lax.rem(block, count), count)
        return pl.multiple_of((holder * per + lax.div(block, count)) * UNIT, UNIT)

    for q in range(total):
        here = where_is(q)
        chunk = q // count
        rows = pl.ds(q * UNIT, UNIT)

        def folded(other, carry):
            there = where_is(other)
            straight = weight_ref[pl.ds(here, UNIT), pl.ds(there, UNIT)].astype(jnp.float32)
            turned = weight_ref[pl.ds(there, UNIT), pl.ds(here, UNIT)].astype(jnp.float32)
            columns = pl.ds(pl.multiple_of(other * UNIT, UNIT), UNIT)
            out_ref[rows, columns] = (straight + turned.T).astype(jnp.bfloat16)
            return carry

        if chunk:
            lax.fori_loop(0, chunk * count, folded, 0)
        for other in range(chunk * count, (chunk + 1) * count):
            there = where_is(other)
            out_ref[rows, other * UNIT : (other + 1) * UNIT] = weight_ref[
                pl.ds(here, UNIT), pl.ds(there, UNIT)
            ]
        if chunk + 1 < per:
            out_ref[rows, (chunk + 1) * count * UNIT :] = jnp.zeros(
                (UNIT, (per - chunk - 1) * count * UNIT), jnp.bfloat16
            )


def fold(weight, count, per):
    return pl.pallas_call(
        functools.partial(fold_kernel, count, per),
        grid=(1,),
        in_specs=[pl.BlockSpec(weight.shape, lambda i: (0, 0))],
        out_specs=pl.BlockSpec(weight.shape, lambda i: (0, 0)),
        out_shape=jax.ShapeDtypeStruct(weight.shape, jnp.bfloat16),
        compiler_params=pltpu.CompilerParams(vmem_limit_bytes=16 * 2**20),
        cost_estimate=pl.CostEstimate(
            flops=weight.size, bytes_accessed=weight.size * 4, transcendentals=0
        ),
        name="fold",
    )(weight)


def weigh_kernel(depth, band, pieces, above, row_start, block_rows, chunk_rows, scale, weight_ref, *refs):
    piece_refs, above_refs = refs[:pieces], refs[pieces : pieces + above]
    before_ref, out_ref, held, mixed, partial, sems = refs[pieces + above :]
    step = pl.program_id(0)
    tiles = band // LANES
    wide = depth * band + beside_width(depth)

    @pl.when(step == 0)
    def _():
        copies = []
        for group, column in ((piece_refs, 0), (above_refs, wide)):
            at = 0
            for ref in group:
                size, width = ref.shape
                into = held.at[pl.ds(at, size), pl.ds(column, width)]
                copies.append(pltpu.make_async_copy(ref, into, sems.at[len(copies)]))
                copies[-1].start()
                at += size
        for copy in copies:
            copy.wait()
        partial[...] = before_ref[...]

    chunk = (row_start + step * block_rows) // chunk_rows
    for c in range(row_start // chunk_rows, held.shape[0] // chunk_rows):
        reach = (c + 1) * chunk_rows

        @pl.when(chunk == c)
        def _():
            mixed[...] = jnp.dot(
                weight_ref[:, :reach], held[:reach], preferred_element_type=jnp.float32
            )

    lane = lane_index((GROUP, LANES))
    left = lane < LANES - NY
    inner = jnp.where(lax.rem(lane, NY) != NY - 1, 1.0, 0.0)
    base = row_start + step * block_rows

    for plane in range(depth):
        beside_tile = depth * band + (plane * NY // LANES) * LANES
        turn = (LANES - NY - plane * NY) % LANES

        def rows_of(group, totals):
            at = pl.ds(pl.multiple_of(group * GROUP, GROUP), GROUP)
            at_held = pl.ds(pl.multiple_of(base + group * GROUP, GROUP), GROUP)

            def read(column):
                lanes = pl.ds(column, LANES)
                return held[at_held, lanes].astype(jnp.float32), mixed[at, lanes]

            centre = [read(plane * band + t * LANES) for t in range(tiles)]
            over = (plane + 1) * band if plane < depth - 1 else wide
            above = [read(over + t * LANES) for t in range(tiles)]
            ahead = [tuple(pltpu.roll(c, LANES - NY, 1) for c in pair) for pair in centre]
            ahead.append(tuple(pltpu.roll(c, turn, 1) if turn else c for c in read(beside_tile)))
            result = []
            for t in range(tiles):
                value, product = centre[t]
                total = (above[t][0] - value) * (above[t][1] - product)
                total = total + (jnp.where(left, ahead[t][0], ahead[t + 1][0]) - value) * (
                    jnp.where(left, ahead[t][1], ahead[t + 1][1]) - product
                )
                total = total + (pltpu.roll(value, LANES - 1, 1) * inner - value) * (
                    pltpu.roll(product, LANES - 1, 1) * inner - product
                )
                result.append(totals[t] + (total[:8] + total[8:]))
            return tuple(result)

        rows = pl.ds(plane * 8, 8)
        start = tuple(partial[rows, t * LANES : (t + 1) * LANES] for t in range(tiles))
        sums = lax.fori_loop(0, block_rows // GROUP, rows_of, start, unroll=4)
        for t in range(tiles):
            partial[rows, t * LANES : (t + 1) * LANES] = sums[t]

    @pl.when(step == pl.num_programs(0) - 1)
    def _():
        if scale is None:
            out_ref[...] = partial[...]
        else:
            for plane in range(depth):
                total = jnp.sum(partial[plane * 8 : plane * 8 + 8, :], axis=0, keepdims=True)
                out_ref[plane : plane + 1, :] = total * scale


def weigh(weight, pieces, above, before, row_start, rows, chunk_rows, depth, band, scale):
    width = pieces[0].shape[1] + band
    held = sum(piece.shape[0] for piece in pieces)
    block_rows = UNIT
    first = row_start // block_rows
    out = (depth, band) if scale is not None else (depth * 8, band)
    return pl.pallas_call(
        functools.partial(
            weigh_kernel, depth, band, len(pieces), len(above), row_start, block_rows, chunk_rows, scale
        ),
        grid=(rows // block_rows,),
        in_specs=[pl.BlockSpec((block_rows, weight.shape[1]), lambda i: (i + first, 0))]
        + [pl.BlockSpec(memory_space=pl.ANY)] * (len(pieces) + len(above))
        + [pl.BlockSpec((depth * 8, band), lambda i: (0, 0))],
        out_specs=pl.BlockSpec(out, lambda i: (0, 0)),
        out_shape=jax.ShapeDtypeStruct(out, jnp.float32),
        scratch_shapes=[
            pltpu.VMEM((held, width), jnp.bfloat16),
            pltpu.VMEM((block_rows, width), jnp.float32),
            pltpu.VMEM((depth * 8, band), jnp.float32),
            pltpu.SemaphoreType.DMA((len(pieces) + len(above),)),
        ],
        compiler_params=pltpu.CompilerParams(vmem_limit_bytes=32 * 2**20),
        cost_estimate=pl.CostEstimate(
            flops=2 * rows * held * width, bytes_accessed=2 * held * width, transcendentals=0
        ),
        name="weigh",
    )(weight, *pieces, *above, before)


def body(conductivity, prev_fields, electrodes, data_weight):
    local, depth, cells = prev_fields.shape
    count = lax.axis_size("src")
    band = cells // count
    sources = data_weight.shape[0]
    per = local // UNIT
    halos = []
    for k in range(per):
        own, inner, outer = pack(prev_fields, conductivity, k)
        outer = lax.ppermute(outer, "cells", pairs_of("cells", 1))
        inner = lax.ppermute(inner, "cells", pairs_of("cells", 0))
        halos.append((own, inner, outer))
    coefs = stencil_coefficients(conductivity, *halos[0][1:], depth * lax.axis_size("cells"))
    weight = fold(data_weight, count, per)
    down = [(i + 1, i) for i in range(lax.axis_size("cells") - 1)]
    stops = [stop for stop in (per - 2, per - 1, per) if stop > 0]
    potentials = None
    pieces, above = [], []
    sums = jnp.zeros((depth * 8, band), jnp.float32)
    done = 0
    for k in range(per):
        potentials, kept, *sent = sweep(
            *halos[k], coefs, electrodes, potentials, local, k * UNIT, count, band
        )
        pieces.append(kept)
        for r in range(1, count):
            pairs = [(i, (i + r) % count) for i in range(count)]
            pieces.append(lax.ppermute(sent[r - 1], "src", pairs))
    for stop in stops:
        lowest = jnp.concatenate([p[:, :band] for p in pieces[done * count : stop * count]], axis=0)
        above.append(lax.ppermute(lowest, "cells", down))
        sums = weigh(
            weight,
            pieces[: stop * count],
            above,
            sums,
            done * UNIT * count,
            (stop - done) * UNIT * count,
            UNIT * count,
            depth,
            band,
            1.0 / sources if stop == per else None,
        )
        done = stop
    return (potentials, sums)


def solution(mesh):
    placed = (P("cells", None), P("src", "cells", None), P("src", None), P())
    return jax.shard_map(
        body,
        mesh=mesh,
        in_specs=placed,
        out_specs=(P("src", "cells", None), P("cells", "src")),
        check_vma=False,
    )
```

```python
import functools

import jax
import jax.numpy as jnp
from jax import lax
from jax.experimental import pallas as pl
from jax.experimental.pallas import tpu as pltpu
from jax.sharding import PartitionSpec as P


NY = 32
current = 4.0
LANES = 128
GROUP = 16
ROWS = 32
UNIT = 128
HALO = 2
PART = 16


def pairs_of(axis, first):
    count = lax.axis_size(axis)
    pairs = [(i, i + 1) for i in range(first, count - 1, 2)]
    return pairs + [(b, a) for a, b in pairs]


def coefficient_kernel(depth, planes_total, sigma_ref, inner_ref, outer_ref, out_ref, padded):
    cells = sigma_ref.shape[1]
    planes = depth + 2
    slab = lax.axis_index("cells")
    odd = lax.rem(slab, 2)

    def put(at, ref):
        for i in range(HALO):
            part = ref[i].astype(jnp.float32)
            padded[at + i : at + i + 1, :] = (part[2:3] + part[1:2]) + part[0:1]

    padded[HALO : HALO + depth, :] = sigma_ref[...]

    @pl.when(odd == 0)
    def _():
        put(0, outer_ref)
        put(HALO + depth, inner_ref)

    @pl.when(odd == 1)
    def _():
        put(0, inner_ref)
        put(HALO + depth, outer_ref)

    sigma = padded[1 : planes + 1, :]
    column = lax.broadcasted_iota(jnp.int32, sigma.shape, 1)
    row = lax.rem(column, NY)
    plane = slab * depth - 1 + lax.broadcasted_iota(jnp.int32, sigma.shape, 0)
    inside = (plane >= 0) & (plane < planes_total)
    zero = jnp.zeros_like(sigma)
    upper, lower = row != NY - 1, row != 0
    ahead, behind = column < cells - NY, column >= NY
    z_plus = 0.5 * (sigma + padded[2 : planes + 2, :])
    z_minus = 0.5 * (sigma + padded[0:planes, :])
    y_plus = 0.5 * (sigma + jnp.where(upper, pltpu.roll(sigma, cells - 1, 1), zero))
    y_minus = 0.5 * (sigma + jnp.where(lower, pltpu.roll(sigma, 1, 1), zero))
    x_plus = 0.5 * (sigma + jnp.where(ahead, pltpu.roll(sigma, cells - NY, 1), zero))
    x_minus = 0.5 * (sigma + jnp.where(behind, pltpu.roll(sigma, NY, 1), zero))
    diagonal = z_plus + z_minus + y_plus + y_minus + x_plus + x_minus
    scale = jnp.where(inside, 2.0 / jnp.where(inside, diagonal, 1.0), zero)
    kinds = [
        z_plus * scale,
        z_minus * scale,
        jnp.where(upper, y_plus * scale, zero),
        jnp.where(lower, y_minus * scale, zero),
        jnp.where(ahead, x_plus * scale, zero),
        jnp.where(behind, x_minus * scale, zero),
        current * scale,
        -current * scale,
    ]
    for kind, values in enumerate(kinds):
        for i in range(planes):
            out_ref[i, kind : kind + 1, :] = values[i : i + 1, :]


def stencil_coefficients(conductivity, inner, outer, planes_total):
    depth, cells = conductivity.shape
    part = inner.shape[1] // PART - 1
    shape = (depth + 2, 8, cells)
    return pl.pallas_call(
        functools.partial(coefficient_kernel, depth, planes_total),
        grid=(1,),
        in_specs=[pl.BlockSpec((depth, cells), lambda i: (0, 0))]
        + [pl.BlockSpec((HALO, PART, cells), lambda i: (0, part, 0))] * 2,
        out_specs=pl.BlockSpec(shape, lambda i: (0, 0, 0)),
        out_shape=jax.ShapeDtypeStruct(shape, jnp.float32),
        scratch_shapes=[pltpu.VMEM((2 * HALO + depth, cells), jnp.float32)],
        compiler_params=pltpu.CompilerParams(vmem_limit_bytes=8 * 2**20),
        name="coefficients",
    )(conductivity, inner, outer)


def pack_kernel(extra, fields_ref, sigma_ref, inner_ref, outer_ref):
    rows, depth, cells = fields_ref.shape
    odd = lax.rem(lax.axis_index("cells"), 2)
    turned = jnp.swapaxes(fields_ref[...].astype(jnp.float32), 0, 1).astype(jnp.bfloat16)

    def part(plane):
        rest = jnp.broadcast_to(sigma_ref[plane : plane + 1, :], (PART, cells))
        row = lax.broadcasted_iota(jnp.int32, rest.shape, 0)
        parts = jnp.zeros_like(rest)
        for i in range(3):
            rounded = rest.astype(jnp.bfloat16).astype(jnp.float32)
            parts = jnp.where(row == i, rounded, parts)
            rest = rest - rounded
        return parts.astype(jnp.bfloat16)

    def pick(out_ref, start):
        out_ref[:, 0:rows] = turned[start : start + HALO]
        if extra:
            for i in range(HALO):
                out_ref[i, rows : rows + PART, :] = part(start + i)

    @pl.when(odd == 0)
    def _():
        pick(inner_ref, depth - HALO)
        pick(outer_ref, 0)

    @pl.when(odd == 1)
    def _():
        pick(inner_ref, 0)
        pick(outer_ref, depth - HALO)


def pack(fields, conductivity, k):
    _, depth, cells = fields.shape
    extra = k == 0
    rows = UNIT if extra else ROWS
    steps = UNIT // rows
    sent = UNIT + (PART if extra else 0)
    block = sent if extra else rows
    return pl.pallas_call(
        functools.partial(pack_kernel, extra),
        grid=(steps,),
        in_specs=[
            pl.BlockSpec((rows, depth, cells), lambda i: (i + k * steps, 0, 0)),
            pl.BlockSpec((depth, cells), lambda i: (0, 0)),
        ],
        out_specs=[pl.BlockSpec((HALO, block, cells), lambda i: (0, i, 0))] * 2,
        out_shape=[jax.ShapeDtypeStruct((HALO, sent, cells), jnp.bfloat16)] * 2,
        compiler_params=pltpu.CompilerParams(vmem_limit_bytes=60 * 2**20),
        name="pack",
    )(fields, conductivity)


def lane_index(shape):
    return lax.broadcasted_iota(jnp.int32, shape, 1)


def sweep_kernel(count, band, own_ref, inner_ref, outer_ref, coef_ref, elec_ref, *refs):
    refs = refs[-(count + 6) :]
    pot_ref, outs, (first, second, extra, final) = refs[0], refs[1 : count + 1], refs[count + 1 : count + 5]
    elec_b = refs[count + 5]
    rows, depth, cells = own_ref.shape
    slab = lax.axis_index("cells")
    odd = lax.rem(slab, 2)
    tiles = cells // LANES
    turned = jnp.swapaxes(own_ref[...].astype(jnp.float32), 0, 1)
    first[HALO : HALO + depth] = turned.astype(jnp.bfloat16)

    @pl.when(odd == 0)
    def _():
        first[0:HALO] = outer_ref[...]
        first[HALO + depth :] = inner_ref[...]

    @pl.when(odd == 1)
    def _():
        first[0:HALO] = inner_ref[...]
        first[HALO + depth :] = outer_ref[...]

    elec_b[0] = jnp.broadcast_to(elec_ref[:, 0:1], (rows, LANES))
    elec_b[1] = jnp.broadcast_to(elec_ref[:, 1:2], (rows, LANES))
    lane = lane_index((GROUP, LANES))
    left = lane < LANES - NY
    right = lane >= NY
    groups = rows // GROUP

    def spread(row):
        return jnp.broadcast_to(row, (GROUP, LANES))

    def stencil(source, plane, coef_plane, at):
        centre = [source[plane, at, pl.ds(v * LANES, LANES)].astype(jnp.float32) for v in range(tiles)]
        ahead = [pltpu.roll(c, LANES - NY, 1) for c in centre]
        behind = [pltpu.roll(c, NY, 1) for c in centre]

        def tile(v):
            lanes = pl.ds(v * LANES, LANES)

            def coef(kind):
                return spread(coef_ref[coef_plane, kind : kind + 1, lanes])

            x_plus = ahead[v] if v == tiles - 1 else jnp.where(left, ahead[v], ahead[v + 1])
            x_minus = behind[v] if v == 0 else jnp.where(right, behind[v], behind[v - 1])
            total = centre[v] + coef(0) * source[plane + 1, at, lanes].astype(jnp.float32)
            side = coef(1) * source[plane - 1, at, lanes].astype(jnp.float32)
            total = total + coef(2) * pltpu.roll(centre[v], LANES - 1, 1)
            side = side + coef(3) * pltpu.roll(centre[v], 1, 1)
            total = total + coef(4) * x_plus
            side = side + coef(5) * x_minus
            return total + side

        return tile

    def relax_first(plane, at):
        sums = stencil(first, plane + 1, plane, at)
        base = (slab * depth + plane - 1) * cells
        plus = elec_b[0, at, :] - base
        minus = elec_b[1, at, :] - base

        def tile(v):
            lanes = pl.ds(v * LANES, LANES)
            strength = spread(coef_ref[plane, 6:7, lanes])
            negative = spread(coef_ref[plane, 7:8, lanes])
            here = lane + v * LANES
            added = jnp.where(plus == here, strength, jnp.where(minus == here, negative, 0.0))
            extra[plane, at, lanes] = added
            second[plane, at, lanes] = sums(v) + added

        return tile

    def relax_second(plane, at):
        sums = stencil(second, plane + 1, plane + 1, at)

        def tile(v):
            lanes = pl.ds(v * LANES, LANES)
            value = sums(v) * (1.0 / 9.0) + extra[plane + 1, at, lanes] * (1.0 / 3.0)
            final[plane, at, lanes] = value.astype(jnp.bfloat16)

        return tile

    spans = [pl.ds(group * GROUP, GROUP) for group in range(groups)]

    def run(makers):
        works = [make() for make in makers]
        for v in range(tiles):
            for work in works:
                work(v)

    def only_first(plane, carry):
        for at in spans:
            run([lambda: relax_first(plane, at)])
        return carry

    def both(plane, carry):
        for at in spans:
            run([lambda: relax_second(plane - 3, at), lambda: relax_first(plane, at)])
        return carry

    planes = depth + 2
    lax.fori_loop(0, 3, only_first, 0)
    lax.fori_loop(3, planes, both, 0)
    for plane in range(planes - 3, depth):
        for at in spans:
            run([lambda: relax_second(plane, at)])
    pot_ref[...] = jnp.swapaxes(final[...].astype(jnp.float32), 0, 1).astype(jnp.bfloat16)

    wide = lane_index((rows, LANES))
    for r in range(count):
        out = outs[r]
        target = lax.rem(lax.axis_index("src") + r, count)
        start = pl.multiple_of(target * band, LANES)
        for plane in range(depth):
            out[:, plane * band : (plane + 1) * band] = final[plane, :, pl.ds(start, band)]
        after = jnp.minimum(target + 1, count - 1)
        after_start = pl.multiple_of(after * band, LANES)
        kept = (target < count - 1).astype(jnp.float32)
        for piece in range(beside_width(depth) // LANES):
            packed = jnp.zeros((rows, LANES), jnp.float32)
            for slot in range(LANES // NY):
                plane = piece * (LANES // NY) + slot
                if plane < depth:
                    row = final[plane, :, pl.ds(after_start, LANES)].astype(jnp.float32)
                    row = pltpu.roll(row, slot * NY, 1) if slot else row
                    mine = (wide >= slot * NY) & (wide < (slot + 1) * NY)
                    packed = jnp.where(mine, row, packed)
            begin = depth * band + piece * LANES
            out[:, begin : begin + LANES] = (packed * kept).astype(jnp.bfloat16)


def beside_width(depth):
    return -(-depth * NY // LANES) * LANES


def sweep(fields, inner, outer, coefs, electrodes, before, begin, size, count, band):
    total, depth, cells = fields.shape
    width = depth * band + beside_width(depth)
    block = begin // ROWS
    in_specs = [
        pl.BlockSpec((ROWS, depth, cells), lambda i: (i + block, 0, 0)),
        pl.BlockSpec((HALO, ROWS, cells), lambda i: (0, i, 0)),
        pl.BlockSpec((HALO, ROWS, cells), lambda i: (0, i, 0)),
        pl.BlockSpec(coefs.shape, lambda i: (0, 0, 0)),
        pl.BlockSpec((ROWS, 2), lambda i: (i + block, 0)),
    ]
    args = [fields, inner, outer, coefs, electrodes]
    aliases = {}
    if before is not None:
        in_specs.append(pl.BlockSpec(memory_space=pl.ANY))
        args.append(before)
        aliases = {5: 0}
    planes = depth + 2
    return pl.pallas_call(
        functools.partial(sweep_kernel, count, band),
        grid=(size // ROWS,),
        in_specs=in_specs,
        out_specs=[pl.BlockSpec((ROWS, depth, cells), lambda i: (i + block, 0, 0))]
        + [pl.BlockSpec((ROWS, width), lambda i: (i, 0))] * count,
        scratch_shapes=[
            pltpu.VMEM((2 * HALO + depth, ROWS, cells), jnp.bfloat16),
            pltpu.VMEM((planes, ROWS, cells), jnp.float32),
            pltpu.VMEM((planes, ROWS, cells), jnp.float32),
            pltpu.VMEM((depth, ROWS, cells), jnp.bfloat16),
            pltpu.VMEM((2, ROWS, LANES), jnp.int32),
        ],
        out_shape=[jax.ShapeDtypeStruct((total, depth, cells), jnp.bfloat16)]
        + [jax.ShapeDtypeStruct((size, width), jnp.bfloat16)] * count,
        input_output_aliases=aliases,
        compiler_params=pltpu.CompilerParams(vmem_limit_bytes=60 * 2**20),
        cost_estimate=pl.CostEstimate(
            flops=size * cells * planes * 40,
            bytes_accessed=size * cells * 2 * (3 * depth + 2 * HALO),
            transcendentals=0,
        ),
        name="sweep",
    )(*args)


def fold_kernel(count, per, weight_ref, out_ref):
    total = count * per

    def where_is(block):
        holder = lax.rem(lax.axis_index("src") + count - lax.rem(block, count), count)
        return pl.multiple_of((holder * per + lax.div(block, count)) * UNIT, UNIT)

    for q in range(total):
        here = where_is(q)
        chunk = q // count
        rows = pl.ds(q * UNIT, UNIT)

        def folded(other, carry):
            there = where_is(other)
            straight = weight_ref[pl.ds(here, UNIT), pl.ds(there, UNIT)].astype(jnp.float32)
            turned = weight_ref[pl.ds(there, UNIT), pl.ds(here, UNIT)].astype(jnp.float32)
            columns = pl.ds(pl.multiple_of(other * UNIT, UNIT), UNIT)
            out_ref[rows, columns] = (straight + turned.T).astype(jnp.bfloat16)
            return carry

        if chunk:
            lax.fori_loop(0, chunk * count, folded, 0)
        for other in range(chunk * count, (chunk + 1) * count):
            there = where_is(other)
            out_ref[rows, other * UNIT : (other + 1) * UNIT] = weight_ref[
                pl.ds(here, UNIT), pl.ds(there, UNIT)
            ]
        if chunk + 1 < per:
            out_ref[rows, (chunk + 1) * count * UNIT :] = jnp.zeros(
                (UNIT, (per - chunk - 1) * count * UNIT), jnp.bfloat16
            )


def fold(weight, count, per):
    return pl.pallas_call(
        functools.partial(fold_kernel, count, per),
        grid=(1,),
        in_specs=[pl.BlockSpec(weight.shape, lambda i: (0, 0))],
        out_specs=pl.BlockSpec(weight.shape, lambda i: (0, 0)),
        out_shape=jax.ShapeDtypeStruct(weight.shape, jnp.bfloat16),
        compiler_params=pltpu.CompilerParams(vmem_limit_bytes=16 * 2**20),
        cost_estimate=pl.CostEstimate(
            flops=weight.size, bytes_accessed=weight.size * 4, transcendentals=0
        ),
        name="fold",
    )(weight)


def weigh_kernel(depth, band, pieces, above, row_start, block_rows, chunk_rows, scale, weight_ref, *refs):
    piece_refs, above_refs = refs[:pieces], refs[pieces : pieces + above]
    before_ref, out_ref, held, mixed, partial, sems = refs[pieces + above :]
    step = pl.program_id(0)
    tiles = band // LANES
    wide = depth * band + beside_width(depth)

    @pl.when(step == 0)
    def _():
        copies = []
        for group, column in ((piece_refs, 0), (above_refs, wide)):
            at = 0
            for ref in group:
                size, width = ref.shape
                into = held.at[pl.ds(at, size), pl.ds(column, width)]
                copies.append(pltpu.make_async_copy(ref, into, sems.at[len(copies)]))
                copies[-1].start()
                at += size
        for copy in copies:
            copy.wait()
        partial[...] = before_ref[...]

    chunk = (row_start + step * block_rows) // chunk_rows
    for c in range(row_start // chunk_rows, held.shape[0] // chunk_rows):
        reach = (c + 1) * chunk_rows

        @pl.when(chunk == c)
        def _():
            mixed[...] = jnp.dot(
                weight_ref[:, :reach], held[:reach], preferred_element_type=jnp.float32
            )

    lane = lane_index((GROUP, LANES))
    left = lane < LANES - NY
    inner = jnp.where(lax.rem(lane, NY) != NY - 1, 1.0, 0.0)
    base = row_start + step * block_rows

    for plane in range(depth):
        beside_tile = depth * band + (plane * NY // LANES) * LANES
        turn = (LANES - NY - plane * NY) % LANES

        def rows_of(group, totals):
            at = pl.ds(pl.multiple_of(group * GROUP, GROUP), GROUP)
            at_held = pl.ds(pl.multiple_of(base + group * GROUP, GROUP), GROUP)

            def read(column):
                lanes = pl.ds(column, LANES)
                return held[at_held, lanes].astype(jnp.float32), mixed[at, lanes]

            centre = [read(plane * band + t * LANES) for t in range(tiles)]
            over = (plane + 1) * band if plane < depth - 1 else wide
            above = [read(over + t * LANES) for t in range(tiles)]
            ahead = [tuple(pltpu.roll(c, LANES - NY, 1) for c in pair) for pair in centre]
            ahead.append(tuple(pltpu.roll(c, turn, 1) if turn else c for c in read(beside_tile)))
            result = []
            for t in range(tiles):
                value, product = centre[t]
                total = (above[t][0] - value) * (above[t][1] - product)
                total = total + (jnp.where(left, ahead[t][0], ahead[t + 1][0]) - value) * (
                    jnp.where(left, ahead[t][1], ahead[t + 1][1]) - product
                )
                total = total + (pltpu.roll(value, LANES - 1, 1) * inner - value) * (
                    pltpu.roll(product, LANES - 1, 1) * inner - product
                )
                result.append(totals[t] + (total[:8] + total[8:]))
            return tuple(result)

        rows = pl.ds(plane * 8, 8)
        start = tuple(partial[rows, t * LANES : (t + 1) * LANES] for t in range(tiles))
        sums = lax.fori_loop(0, block_rows // GROUP, rows_of, start, unroll=4)
        for t in range(tiles):
            partial[rows, t * LANES : (t + 1) * LANES] = sums[t]

    @pl.when(step == pl.num_programs(0) - 1)
    def _():
        if scale is None:
            out_ref[...] = partial[...]
        else:
            for plane in range(depth):
                total = jnp.sum(partial[plane * 8 : plane * 8 + 8, :], axis=0, keepdims=True)
                out_ref[plane : plane + 1, :] = total * scale


def weigh(weight, pieces, above, before, row_start, rows, chunk_rows, depth, band, scale):
    width = pieces[0].shape[1] + band
    held = sum(piece.shape[0] for piece in pieces)
    block_rows = UNIT
    first = row_start // block_rows
    out = (depth, band) if scale is not None else (depth * 8, band)
    return pl.pallas_call(
        functools.partial(
            weigh_kernel, depth, band, len(pieces), len(above), row_start, block_rows, chunk_rows, scale
        ),
        grid=(rows // block_rows,),
        in_specs=[pl.BlockSpec((block_rows, weight.shape[1]), lambda i: (i + first, 0))]
        + [pl.BlockSpec(memory_space=pl.ANY)] * (len(pieces) + len(above))
        + [pl.BlockSpec((depth * 8, band), lambda i: (0, 0))],
        out_specs=pl.BlockSpec(out, lambda i: (0, 0)),
        out_shape=jax.ShapeDtypeStruct(out, jnp.float32),
        scratch_shapes=[
            pltpu.VMEM((held, width), jnp.bfloat16),
            pltpu.VMEM((block_rows, width), jnp.float32),
            pltpu.VMEM((depth * 8, band), jnp.float32),
            pltpu.SemaphoreType.DMA((len(pieces) + len(above),)),
        ],
        compiler_params=pltpu.CompilerParams(vmem_limit_bytes=32 * 2**20),
        cost_estimate=pl.CostEstimate(
            flops=2 * rows * held * width, bytes_accessed=2 * held * width, transcendentals=0
        ),
        name="weigh",
    )(weight, *pieces, *above, before)


def body(conductivity, prev_fields, electrodes, data_weight):
    local, depth, cells = prev_fields.shape
    count = lax.axis_size("src")
    band = cells // count
    sources = data_weight.shape[0]
    per = local // UNIT
    halos = []
    for k in range(per):
        inner, outer = pack(prev_fields, conductivity, k)
        outer = lax.ppermute(outer, "cells", pairs_of("cells", 1))
        inner = lax.ppermute(inner, "cells", pairs_of("cells", 0))
        halos.append((inner, outer))
    coefs = stencil_coefficients(conductivity, *halos[0], depth * lax.axis_size("cells"))
    weight = fold(data_weight, count, per)
    down = [(i + 1, i) for i in range(lax.axis_size("cells") - 1)]
    stops = [stop for stop in (per - 2, per - 1, per) if stop > 0]
    potentials = None
    pieces, above = [], []
    sums = jnp.zeros((depth * 8, band), jnp.float32)
    done = 0
    for k in range(per):
        potentials, kept, *sent = sweep(
            prev_fields, *halos[k], coefs, electrodes, potentials, k * UNIT, UNIT, count, band
        )
        pieces.append(kept)
        for r in range(1, count):
            pairs = [(i, (i + r) % count) for i in range(count)]
            pieces.append(lax.ppermute(sent[r - 1], "src", pairs))
    for stop in stops:
        lowest = jnp.concatenate([p[:, :band] for p in pieces[done * count : stop * count]], axis=0)
        above.append(lax.ppermute(lowest, "cells", down))
        sums = weigh(
            weight,
            pieces[: stop * count],
            above,
            sums,
            done * UNIT * count,
            (stop - done) * UNIT * count,
            UNIT * count,
            depth,
            band,
            1.0 / sources if stop == per else None,
        )
        done = stop
    return (potentials, sums)


def solution(mesh):
    placed = (P("cells", None), P("src", "cells", None), P("src", None), P())
    return jax.shard_map(
        body,
        mesh=mesh,
        in_specs=placed,
        out_specs=(P("src", "cells", None), P("cells", "src")),
        check_vma=False,
    )
```

```python
import functools

import jax
import jax.numpy as jnp
from jax import lax
from jax.experimental import pallas as pl
from jax.experimental.pallas import tpu as pltpu
from jax.sharding import PartitionSpec as P


NY = 32
current = 4.0
LANES = 128
GROUP = 16
ROWS = 32
UNIT = 128
HALO = 2
PART = 16


def pairs_of(axis, first):
    count = lax.axis_size(axis)
    pairs = [(i, i + 1) for i in range(first, count - 1, 2)]
    return pairs + [(b, a) for a, b in pairs]


def coefficient_kernel(depth, planes_total, sigma_ref, inner_ref, outer_ref, out_ref, padded):
    cells = sigma_ref.shape[1]
    planes = depth + 2
    slab = lax.axis_index("cells")
    odd = lax.rem(slab, 2)

    def put(at, ref):
        for i in range(HALO):
            part = ref[i].astype(jnp.float32)
            padded[at + i : at + i + 1, :] = (part[2:3] + part[1:2]) + part[0:1]

    padded[HALO : HALO + depth, :] = sigma_ref[...]

    @pl.when(odd == 0)
    def _():
        put(0, outer_ref)
        put(HALO + depth, inner_ref)

    @pl.when(odd == 1)
    def _():
        put(0, inner_ref)
        put(HALO + depth, outer_ref)

    sigma = padded[1 : planes + 1, :]
    column = lax.broadcasted_iota(jnp.int32, sigma.shape, 1)
    row = lax.rem(column, NY)
    plane = slab * depth - 1 + lax.broadcasted_iota(jnp.int32, sigma.shape, 0)
    inside = (plane >= 0) & (plane < planes_total)
    zero = jnp.zeros_like(sigma)
    upper, lower = row != NY - 1, row != 0
    ahead, behind = column < cells - NY, column >= NY
    z_plus = 0.5 * (sigma + padded[2 : planes + 2, :])
    z_minus = 0.5 * (sigma + padded[0:planes, :])
    y_plus = 0.5 * (sigma + jnp.where(upper, pltpu.roll(sigma, cells - 1, 1), zero))
    y_minus = 0.5 * (sigma + jnp.where(lower, pltpu.roll(sigma, 1, 1), zero))
    x_plus = 0.5 * (sigma + jnp.where(ahead, pltpu.roll(sigma, cells - NY, 1), zero))
    x_minus = 0.5 * (sigma + jnp.where(behind, pltpu.roll(sigma, NY, 1), zero))
    diagonal = z_plus + z_minus + y_plus + y_minus + x_plus + x_minus
    scale = jnp.where(inside, 2.0 / jnp.where(inside, diagonal, 1.0), zero)
    kinds = [
        z_plus * scale,
        z_minus * scale,
        jnp.where(upper, y_plus * scale, zero),
        jnp.where(lower, y_minus * scale, zero),
        jnp.where(ahead, x_plus * scale, zero),
        jnp.where(behind, x_minus * scale, zero),
        current * scale,
        -current * scale,
    ]
    for kind, values in enumerate(kinds):
        for i in range(planes):
            out_ref[i, kind : kind + 1, :] = values[i : i + 1, :]


def stencil_coefficients(conductivity, inner, outer, planes_total):
    depth, cells = conductivity.shape
    part = inner.shape[1] // PART - 1
    shape = (depth + 2, 8, cells)
    return pl.pallas_call(
        functools.partial(coefficient_kernel, depth, planes_total),
        grid=(1,),
        in_specs=[pl.BlockSpec((depth, cells), lambda i: (0, 0))]
        + [pl.BlockSpec((HALO, PART, cells), lambda i: (0, part, 0))] * 2,
        out_specs=pl.BlockSpec(shape, lambda i: (0, 0, 0)),
        out_shape=jax.ShapeDtypeStruct(shape, jnp.float32),
        scratch_shapes=[pltpu.VMEM((2 * HALO + depth, cells), jnp.float32)],
        compiler_params=pltpu.CompilerParams(vmem_limit_bytes=8 * 2**20),
        name="coefficients",
    )(conductivity, inner, outer)


def pack_kernel(extra, fields_ref, sigma_ref, own_ref, inner_ref, outer_ref):
    rows, depth, cells = fields_ref.shape
    odd = lax.rem(lax.axis_index("cells"), 2)
    own_ref[...] = jnp.swapaxes(fields_ref[...].astype(jnp.float32), 0, 1).astype(jnp.bfloat16)

    def part(plane):
        rest = jnp.broadcast_to(sigma_ref[plane : plane + 1, :], (PART, cells))
        row = lax.broadcasted_iota(jnp.int32, rest.shape, 0)
        parts = jnp.zeros_like(rest)
        for i in range(3):
            rounded = rest.astype(jnp.bfloat16).astype(jnp.float32)
            parts = jnp.where(row == i, rounded, parts)
            rest = rest - rounded
        return parts.astype(jnp.bfloat16)

    def pick(out_ref, start):
        out_ref[:, 0:rows] = own_ref[start : start + HALO]
        if extra:
            for i in range(HALO):
                out_ref[i, rows : rows + PART, :] = part(start + i)

    @pl.when(odd == 0)
    def _():
        pick(inner_ref, depth - HALO)
        pick(outer_ref, 0)

    @pl.when(odd == 1)
    def _():
        pick(inner_ref, 0)
        pick(outer_ref, depth - HALO)


def pack(fields, conductivity, k):
    _, depth, cells = fields.shape
    extra = k == 0
    rows = UNIT
    steps = UNIT // rows
    sent = UNIT + (PART if extra else 0)
    block = sent
    return pl.pallas_call(
        functools.partial(pack_kernel, extra),
        grid=(steps,),
        in_specs=[
            pl.BlockSpec((rows, depth, cells), lambda i: (i + k * steps, 0, 0)),
            pl.BlockSpec((depth, cells), lambda i: (0, 0)),
        ],
        out_specs=[pl.BlockSpec((depth, rows, cells), lambda i: (0, i, 0))]
        + [pl.BlockSpec((HALO, block, cells), lambda i: (0, i, 0))] * 2,
        out_shape=[jax.ShapeDtypeStruct((depth, UNIT, cells), jnp.bfloat16)]
        + [jax.ShapeDtypeStruct((HALO, sent, cells), jnp.bfloat16)] * 2,
        compiler_params=pltpu.CompilerParams(vmem_limit_bytes=60 * 2**20),
        name="pack",
    )(fields, conductivity)


def lane_index(shape):
    return lax.broadcasted_iota(jnp.int32, shape, 1)


def sweep_kernel(count, band, own_ref, inner_ref, outer_ref, coef_ref, elec_ref, *refs):
    refs = refs[-(count + 6) :]
    pot_ref, outs, (first, second, extra, final) = refs[0], refs[1 : count + 1], refs[count + 1 : count + 5]
    elec_b = refs[count + 5]
    depth, rows, cells = own_ref.shape
    slab = lax.axis_index("cells")
    odd = lax.rem(slab, 2)
    tiles = cells // LANES
    first[HALO : HALO + depth] = own_ref[...]

    @pl.when(odd == 0)
    def _():
        first[0:HALO] = outer_ref[...]
        first[HALO + depth :] = inner_ref[...]

    @pl.when(odd == 1)
    def _():
        first[0:HALO] = inner_ref[...]
        first[HALO + depth :] = outer_ref[...]

    elec_b[0] = jnp.broadcast_to(elec_ref[:, 0:1], (rows, LANES))
    elec_b[1] = jnp.broadcast_to(elec_ref[:, 1:2], (rows, LANES))
    lane = lane_index((GROUP, LANES))
    left = lane < LANES - NY
    right = lane >= NY
    groups = rows // GROUP

    def spread(row):
        return jnp.broadcast_to(row, (GROUP, LANES))

    def stencil(source, plane, coef_plane, at):
        centre = [source[plane, at, pl.ds(v * LANES, LANES)].astype(jnp.float32) for v in range(tiles)]
        ahead = [pltpu.roll(c, LANES - NY, 1) for c in centre]
        behind = [pltpu.roll(c, NY, 1) for c in centre]

        def tile(v):
            lanes = pl.ds(v * LANES, LANES)

            def coef(kind):
                return spread(coef_ref[coef_plane, kind : kind + 1, lanes])

            x_plus = ahead[v] if v == tiles - 1 else jnp.where(left, ahead[v], ahead[v + 1])
            x_minus = behind[v] if v == 0 else jnp.where(right, behind[v], behind[v - 1])
            total = centre[v] + coef(0) * source[plane + 1, at, lanes].astype(jnp.float32)
            side = coef(1) * source[plane - 1, at, lanes].astype(jnp.float32)
            total = total + coef(2) * pltpu.roll(centre[v], LANES - 1, 1)
            side = side + coef(3) * pltpu.roll(centre[v], 1, 1)
            total = total + coef(4) * x_plus
            side = side + coef(5) * x_minus
            return total + side

        return tile

    def relax_first(plane, at):
        sums = stencil(first, plane + 1, plane, at)
        base = (slab * depth + plane - 1) * cells
        plus = elec_b[0, at, :] - base
        minus = elec_b[1, at, :] - base

        def tile(v):
            lanes = pl.ds(v * LANES, LANES)
            strength = spread(coef_ref[plane, 6:7, lanes])
            negative = spread(coef_ref[plane, 7:8, lanes])
            here = lane + v * LANES
            added = jnp.where(plus == here, strength, jnp.where(minus == here, negative, 0.0))
            extra[plane, at, lanes] = added
            second[plane, at, lanes] = sums(v) + added

        return tile

    def relax_second(plane, at):
        sums = stencil(second, plane + 1, plane + 1, at)

        def tile(v):
            lanes = pl.ds(v * LANES, LANES)
            value = sums(v) * (1.0 / 9.0) + extra[plane + 1, at, lanes] * (1.0 / 3.0)
            final[plane, at, lanes] = value.astype(jnp.bfloat16)

        return tile

    spans = [pl.ds(group * GROUP, GROUP) for group in range(groups)]

    def run(makers):
        works = [make() for make in makers]
        for v in range(tiles):
            for work in works:
                work(v)

    def only_first(plane, carry):
        for at in spans:
            run([lambda: relax_first(plane, at)])
        return carry

    def both(plane, carry):
        for at in spans:
            run([lambda: relax_second(plane - 3, at), lambda: relax_first(plane, at)])
        return carry

    planes = depth + 2
    lax.fori_loop(0, 3, only_first, 0)
    lax.fori_loop(3, planes, both, 0)
    for plane in range(planes - 3, depth):
        for at in spans:
            run([lambda: relax_second(plane, at)])
    pot_ref[...] = jnp.swapaxes(final[...].astype(jnp.float32), 0, 1).astype(jnp.bfloat16)

    wide = lane_index((rows, LANES))
    for r in range(count):
        out = outs[r]
        target = lax.rem(lax.axis_index("src") + r, count)
        start = pl.multiple_of(target * band, LANES)
        for plane in range(depth):
            out[:, plane * band : (plane + 1) * band] = final[plane, :, pl.ds(start, band)]
        after = jnp.minimum(target + 1, count - 1)
        after_start = pl.multiple_of(after * band, LANES)
        kept = (target < count - 1).astype(jnp.float32)
        for piece in range(beside_width(depth) // LANES):
            packed = jnp.zeros((rows, LANES), jnp.float32)
            for slot in range(LANES // NY):
                plane = piece * (LANES // NY) + slot
                if plane < depth:
                    row = final[plane, :, pl.ds(after_start, LANES)].astype(jnp.float32)
                    row = pltpu.roll(row, slot * NY, 1) if slot else row
                    mine = (wide >= slot * NY) & (wide < (slot + 1) * NY)
                    packed = jnp.where(mine, row, packed)
            begin = depth * band + piece * LANES
            out[:, begin : begin + LANES] = (packed * kept).astype(jnp.bfloat16)


def beside_width(depth):
    return -(-depth * NY // LANES) * LANES


def sweep(own, inner, outer, coefs, electrodes, before, total, begin, count, band):
    depth, size, cells = own.shape
    width = depth * band + beside_width(depth)
    block = begin // ROWS
    in_specs = [
        pl.BlockSpec((depth, ROWS, cells), lambda i: (0, i, 0)),
        pl.BlockSpec((HALO, ROWS, cells), lambda i: (0, i, 0)),
        pl.BlockSpec((HALO, ROWS, cells), lambda i: (0, i, 0)),
        pl.BlockSpec(coefs.shape, lambda i: (0, 0, 0)),
        pl.BlockSpec((ROWS, 2), lambda i: (i + block, 0)),
    ]
    args = [own, inner, outer, coefs, electrodes]
    aliases = {}
    if before is not None:
        in_specs.append(pl.BlockSpec(memory_space=pl.ANY))
        args.append(before)
        aliases = {5: 0}
    planes = depth + 2
    return pl.pallas_call(
        functools.partial(sweep_kernel, count, band),
        grid=(size // ROWS,),
        in_specs=in_specs,
        out_specs=[pl.BlockSpec((ROWS, depth, cells), lambda i: (i + block, 0, 0))]
        + [pl.BlockSpec((ROWS, width), lambda i: (i, 0))] * count,
        scratch_shapes=[
            pltpu.VMEM((2 * HALO + depth, ROWS, cells), jnp.bfloat16),
            pltpu.VMEM((planes, ROWS, cells), jnp.float32),
            pltpu.VMEM((planes, ROWS, cells), jnp.float32),
            pltpu.VMEM((depth, ROWS, cells), jnp.bfloat16),
            pltpu.VMEM((2, ROWS, LANES), jnp.int32),
        ],
        out_shape=[jax.ShapeDtypeStruct((total, depth, cells), jnp.bfloat16)]
        + [jax.ShapeDtypeStruct((size, width), jnp.bfloat16)] * count,
        input_output_aliases=aliases,
        compiler_params=pltpu.CompilerParams(vmem_limit_bytes=44 * 2**20),
        cost_estimate=pl.CostEstimate(
            flops=size * cells * planes * 40,
            bytes_accessed=size * cells * 2 * (3 * depth + 2 * HALO),
            transcendentals=0,
        ),
        name="sweep",
    )(*args)


def fold_kernel(count, per, weight_ref, out_ref):
    total = count * per

    def where_is(block):
        holder = lax.rem(lax.axis_index("src") + count - lax.rem(block, count), count)
        return pl.multiple_of((holder * per + lax.div(block, count)) * UNIT, UNIT)

    for q in range(total):
        here = where_is(q)
        rows = pl.ds(q * UNIT, UNIT)

        def folded(other, carry):
            there = where_is(other)
            straight = weight_ref[pl.ds(here, UNIT), pl.ds(there, UNIT)].astype(jnp.float32)
            turned = weight_ref[pl.ds(there, UNIT), pl.ds(here, UNIT)].astype(jnp.float32)
            columns = pl.ds(pl.multiple_of(other * UNIT, UNIT), UNIT)
            out_ref[rows, columns] = (straight + turned.T).astype(jnp.bfloat16)
            return carry

        if q:
            lax.fori_loop(0, q, folded, 0)
        out_ref[rows, q * UNIT : (q + 1) * UNIT] = weight_ref[pl.ds(here, UNIT), pl.ds(here, UNIT)]
        if q + 1 < total:
            rest = (UNIT, (total - q - 1) * UNIT)
            out_ref[rows, (q + 1) * UNIT :] = jnp.zeros(rest, jnp.bfloat16)


def fold(weight, count, per):
    return pl.pallas_call(
        functools.partial(fold_kernel, count, per),
        grid=(1,),
        in_specs=[pl.BlockSpec(weight.shape, lambda i: (0, 0))],
        out_specs=pl.BlockSpec(weight.shape, lambda i: (0, 0)),
        out_shape=jax.ShapeDtypeStruct(weight.shape, jnp.bfloat16),
        compiler_params=pltpu.CompilerParams(vmem_limit_bytes=16 * 2**20),
        cost_estimate=pl.CostEstimate(
            flops=weight.size, bytes_accessed=weight.size * 4, transcendentals=0
        ),
        name="fold",
    )(weight)


def weigh_kernel(depth, band, pieces, above, row_start, block_rows, scale, weight_ref, *refs):
    piece_refs, above_refs = refs[:pieces], refs[pieces : pieces + above]
    before_ref, out_ref, held, mixed, partial, sems = refs[pieces + above :]
    step = pl.program_id(0)
    tiles = band // LANES
    wide = depth * band + beside_width(depth)

    @pl.when(step == 0)
    def _():
        copies = []
        for group, column in ((piece_refs, 0), (above_refs, wide)):
            at = 0
            for ref in group:
                size, width = ref.shape
                into = held.at[pl.ds(at, size), pl.ds(column, width)]
                copies.append(pltpu.make_async_copy(ref, into, sems.at[len(copies)]))
                copies[-1].start()
                at += size
        for copy in copies:
            copy.wait()
        partial[...] = before_ref[...]

    for c in range(row_start // UNIT, held.shape[0] // UNIT):
        reach = (c + 1) * UNIT

        @pl.when(step == c - row_start // UNIT)
        def _():
            mixed[...] = jnp.dot(
                weight_ref[:, :reach], held[:reach], preferred_element_type=jnp.float32
            )

    lane = lane_index((GROUP, LANES))
    left = lane < LANES - NY
    inner = jnp.where(lax.rem(lane, NY) != NY - 1, 1.0, 0.0)
    base = row_start + step * block_rows

    for plane in range(depth):
        beside_tile = depth * band + (plane * NY // LANES) * LANES
        turn = (LANES - NY - plane * NY) % LANES

        def rows_of(group, totals):
            at = pl.ds(pl.multiple_of(group * GROUP, GROUP), GROUP)
            at_held = pl.ds(pl.multiple_of(base + group * GROUP, GROUP), GROUP)

            def read(column):
                lanes = pl.ds(column, LANES)
                return held[at_held, lanes].astype(jnp.float32), mixed[at, lanes]

            centre = [read(plane * band + t * LANES) for t in range(tiles)]
            over = (plane + 1) * band if plane < depth - 1 else wide
            above = [read(over + t * LANES) for t in range(tiles)]
            ahead = [tuple(pltpu.roll(c, LANES - NY, 1) for c in pair) for pair in centre]
            ahead.append(tuple(pltpu.roll(c, turn, 1) if turn else c for c in read(beside_tile)))
            result = []
            for t in range(tiles):
                value, product = centre[t]
                total = (above[t][0] - value) * (above[t][1] - product)
                total = total + (jnp.where(left, ahead[t][0], ahead[t + 1][0]) - value) * (
                    jnp.where(left, ahead[t][1], ahead[t + 1][1]) - product
                )
                total = total + (pltpu.roll(value, LANES - 1, 1) * inner - value) * (
                    pltpu.roll(product, LANES - 1, 1) * inner - product
                )
                result.append(totals[t] + (total[:8] + total[8:]))
            return tuple(result)

        rows = pl.ds(plane * 8, 8)
        start = tuple(partial[rows, t * LANES : (t + 1) * LANES] for t in range(tiles))
        sums = lax.fori_loop(0, block_rows // GROUP, rows_of, start, unroll=True)
        for t in range(tiles):
            partial[rows, t * LANES : (t + 1) * LANES] = sums[t]

    @pl.when(step == pl.num_programs(0) - 1)
    def _():
        if scale is None:
            out_ref[...] = partial[...]
        else:
            for plane in range(depth):
                total = jnp.sum(partial[plane * 8 : plane * 8 + 8, :], axis=0, keepdims=True)
                out_ref[plane : plane + 1, :] = total * scale


def weigh(weight, pieces, above, before, row_start, rows, depth, band, scale):
    width = pieces[0].shape[1] + band
    held = sum(piece.shape[0] for piece in pieces)
    block_rows = UNIT
    first = row_start // block_rows
    out = (depth, band) if scale is not None else (depth * 8, band)
    return pl.pallas_call(
        functools.partial(
            weigh_kernel, depth, band, len(pieces), len(above), row_start, block_rows, scale
        ),
        grid=(rows // block_rows,),
        in_specs=[pl.BlockSpec((block_rows, weight.shape[1]), lambda i: (i + first, 0))]
        + [pl.BlockSpec(memory_space=pl.ANY)] * (len(pieces) + len(above))
        + [pl.BlockSpec((depth * 8, band), lambda i: (0, 0))],
        out_specs=pl.BlockSpec(out, lambda i: (0, 0)),
        out_shape=jax.ShapeDtypeStruct(out, jnp.float32),
        scratch_shapes=[
            pltpu.VMEM((held, width), jnp.bfloat16),
            pltpu.VMEM((block_rows, width), jnp.float32),
            pltpu.VMEM((depth * 8, band), jnp.float32),
            pltpu.SemaphoreType.DMA((len(pieces) + len(above),)),
        ],
        compiler_params=pltpu.CompilerParams(vmem_limit_bytes=32 * 2**20),
        cost_estimate=pl.CostEstimate(
            flops=2 * rows * held * width, bytes_accessed=2 * held * width, transcendentals=0
        ),
        name="weigh",
    )(weight, *pieces, *above, before)


def body(conductivity, prev_fields, electrodes, data_weight):
    local, depth, cells = prev_fields.shape
    count = lax.axis_size("src")
    band = cells // count
    sources = data_weight.shape[0]
    per = local // UNIT
    halos = []
    for k in range(per):
        own, inner, outer = pack(prev_fields, conductivity, k)
        outer = lax.ppermute(outer, "cells", pairs_of("cells", 1))
        inner = lax.ppermute(inner, "cells", pairs_of("cells", 0))
        halos.append((own, inner, outer))
    coefs = stencil_coefficients(conductivity, *halos[0][1:], depth * lax.axis_size("cells"))
    weight = fold(data_weight, count, per)
    down = [(i + 1, i) for i in range(lax.axis_size("cells") - 1)]
    stops = sorted({max(per - 2, 0) * count, (per - 1) * count + 1, per * count} - {0})
    potentials = None
    pieces, above = [], []
    sums = jnp.zeros((depth * 8, band), jnp.float32)
    done = 0
    for k in range(per):
        potentials, kept, *sent = sweep(
            *halos[k], coefs, electrodes, potentials, local, k * UNIT, count, band
        )
        pieces.append(kept)
        for r in range(1, count):
            pairs = [(i, (i + r) % count) for i in range(count)]
            pieces.append(lax.ppermute(sent[r - 1], "src", pairs))
    for stop in stops:
        lowest = jnp.concatenate([p[:, :band] for p in pieces[done:stop]], axis=0)
        above.append(lax.ppermute(lowest, "cells", down))
        sums = weigh(
            weight,
            pieces[:stop],
            above,
            sums,
            done * UNIT,
            (stop - done) * UNIT,
            depth,
            band,
            1.0 / sources if stop == per * count else None,
        )
        done = stop
    return (potentials, sums)


def solution(mesh):
    placed = (P("cells", None), P("src", "cells", None), P("src", None), P())
    return jax.shard_map(
        body,
        mesh=mesh,
        in_specs=placed,
        out_specs=(P("src", "cells", None), P("cells", "src")),
        check_vma=False,
    )
```

```python
import functools

import jax
import jax.numpy as jnp
from jax import lax
from jax.experimental import pallas as pl
from jax.experimental.pallas import tpu as pltpu
from jax.sharding import PartitionSpec as P


NY = 32
current = 4.0
LANES = 128
GROUP = 16
ROWS = 64
UNIT = 128
HALO = 2
PART = 16


def pairs_of(axis, first):
    count = lax.axis_size(axis)
    pairs = [(i, i + 1) for i in range(first, count - 1, 2)]
    return pairs + [(b, a) for a, b in pairs]


def coefficient_kernel(depth, planes_total, sigma_ref, inner_ref, outer_ref, out_ref, padded):
    cells = sigma_ref.shape[1]
    planes = depth + 2
    slab = lax.axis_index("cells")
    odd = lax.rem(slab, 2)

    def put(at, ref):
        for i in range(HALO):
            part = ref[i].astype(jnp.float32)
            padded[at + i : at + i + 1, :] = (part[2:3] + part[1:2]) + part[0:1]

    padded[HALO : HALO + depth, :] = sigma_ref[...]

    @pl.when(odd == 0)
    def _():
        put(0, outer_ref)
        put(HALO + depth, inner_ref)

    @pl.when(odd == 1)
    def _():
        put(0, inner_ref)
        put(HALO + depth, outer_ref)

    sigma = padded[1 : planes + 1, :]
    column = lax.broadcasted_iota(jnp.int32, sigma.shape, 1)
    row = lax.rem(column, NY)
    plane = slab * depth - 1 + lax.broadcasted_iota(jnp.int32, sigma.shape, 0)
    inside = (plane >= 0) & (plane < planes_total)
    zero = jnp.zeros_like(sigma)
    upper, lower = row != NY - 1, row != 0
    ahead, behind = column < cells - NY, column >= NY
    z_plus = 0.5 * (sigma + padded[2 : planes + 2, :])
    z_minus = 0.5 * (sigma + padded[0:planes, :])
    y_plus = 0.5 * (sigma + jnp.where(upper, pltpu.roll(sigma, cells - 1, 1), zero))
    y_minus = 0.5 * (sigma + jnp.where(lower, pltpu.roll(sigma, 1, 1), zero))
    x_plus = 0.5 * (sigma + jnp.where(ahead, pltpu.roll(sigma, cells - NY, 1), zero))
    x_minus = 0.5 * (sigma + jnp.where(behind, pltpu.roll(sigma, NY, 1), zero))
    diagonal = z_plus + z_minus + y_plus + y_minus + x_plus + x_minus
    scale = jnp.where(inside, 2.0 / jnp.where(inside, diagonal, 1.0), zero)
    kinds = [
        z_plus * scale,
        z_minus * scale,
        jnp.where(upper, y_plus * scale, zero),
        jnp.where(lower, y_minus * scale, zero),
        jnp.where(ahead, x_plus * scale, zero),
        jnp.where(behind, x_minus * scale, zero),
        current * scale,
        -current * scale,
    ]
    for kind, values in enumerate(kinds):
        for i in range(planes):
            out_ref[i, kind : kind + 1, :] = values[i : i + 1, :]


def stencil_coefficients(conductivity, inner, outer, planes_total):
    depth, cells = conductivity.shape
    part = inner.shape[1] // PART - 1
    shape = (depth + 2, 8, cells)
    return pl.pallas_call(
        functools.partial(coefficient_kernel, depth, planes_total),
        grid=(1,),
        in_specs=[pl.BlockSpec((depth, cells), lambda i: (0, 0))]
        + [pl.BlockSpec((HALO, PART, cells), lambda i: (0, part, 0))] * 2,
        out_specs=pl.BlockSpec(shape, lambda i: (0, 0, 0)),
        out_shape=jax.ShapeDtypeStruct(shape, jnp.float32),
        scratch_shapes=[pltpu.VMEM((2 * HALO + depth, cells), jnp.float32)],
        compiler_params=pltpu.CompilerParams(vmem_limit_bytes=8 * 2**20),
        name="coefficients",
    )(conductivity, inner, outer)


def pack_kernel(extra, fields_ref, sigma_ref, own_ref, inner_ref, outer_ref):
    rows, depth, cells = fields_ref.shape
    odd = lax.rem(lax.axis_index("cells"), 2)
    own_ref[...] = jnp.swapaxes(fields_ref[...].astype(jnp.float32), 0, 1).astype(jnp.bfloat16)

    def part(plane):
        rest = jnp.broadcast_to(sigma_ref[plane : plane + 1, :], (PART, cells))
        row = lax.broadcasted_iota(jnp.int32, rest.shape, 0)
        parts = jnp.zeros_like(rest)
        for i in range(3):
            rounded = rest.astype(jnp.bfloat16).astype(jnp.float32)
            parts = jnp.where(row == i, rounded, parts)
            rest = rest - rounded
        return parts.astype(jnp.bfloat16)

    def pick(out_ref, start):
        out_ref[:, 0:rows] = own_ref[start : start + HALO]
        if extra:
            for i in range(HALO):
                out_ref[i, rows : rows + PART, :] = part(start + i)

    @pl.when(odd == 0)
    def _():
        pick(inner_ref, depth - HALO)
        pick(outer_ref, 0)

    @pl.when(odd == 1)
    def _():
        pick(inner_ref, 0)
        pick(outer_ref, depth - HALO)


def pack(fields, conductivity, k):
    _, depth, cells = fields.shape
    extra = k == 0
    rows = UNIT
    steps = UNIT // rows
    sent = UNIT + (PART if extra else 0)
    block = sent
    return pl.pallas_call(
        functools.partial(pack_kernel, extra),
        grid=(steps,),
        in_specs=[
            pl.BlockSpec((rows, depth, cells), lambda i: (i + k * steps, 0, 0)),
            pl.BlockSpec((depth, cells), lambda i: (0, 0)),
        ],
        out_specs=[pl.BlockSpec((depth, rows, cells), lambda i: (0, i, 0))]
        + [pl.BlockSpec((HALO, block, cells), lambda i: (0, i, 0))] * 2,
        out_shape=[jax.ShapeDtypeStruct((depth, UNIT, cells), jnp.bfloat16)]
        + [jax.ShapeDtypeStruct((HALO, sent, cells), jnp.bfloat16)] * 2,
        compiler_params=pltpu.CompilerParams(vmem_limit_bytes=60 * 2**20),
        name="pack",
    )(fields, conductivity)


def lane_index(shape):
    return lax.broadcasted_iota(jnp.int32, shape, 1)


def sweep_kernel(count, band, own_ref, inner_ref, outer_ref, coef_ref, elec_ref, *refs):
    refs = refs[-(count + 6) :]
    pot_ref, outs, (first, second, extra, final) = refs[0], refs[1 : count + 1], refs[count + 1 : count + 5]
    elec_b = refs[count + 5]
    depth, rows, cells = own_ref.shape
    slab = lax.axis_index("cells")
    odd = lax.rem(slab, 2)
    tiles = cells // LANES
    first[HALO : HALO + depth] = own_ref[...]

    @pl.when(odd == 0)
    def _():
        first[0:HALO] = outer_ref[...]
        first[HALO + depth :] = inner_ref[...]

    @pl.when(odd == 1)
    def _():
        first[0:HALO] = inner_ref[...]
        first[HALO + depth :] = outer_ref[...]


    @pl.when(pl.program_id(0) == 0)
    def _():
        for e in range(2):
            line = jnp.broadcast_to(elec_ref[e : e + 1, :].astype(jnp.float32), (LANES, UNIT))
            elec_b[e] = line.T.astype(jnp.int32)

    lane = lane_index((GROUP, LANES))
    left = lane < LANES - NY
    right = lane >= NY
    groups = rows // GROUP

    def spread(row):
        return jnp.broadcast_to(row, (GROUP, LANES))

    def stencil(source, plane, coef_plane, at):
        centre = [source[plane, at, pl.ds(v * LANES, LANES)].astype(jnp.float32) for v in range(tiles)]
        ahead = [pltpu.roll(c, LANES - NY, 1) for c in centre]
        behind = [pltpu.roll(c, NY, 1) for c in centre]

        def tile(v):
            lanes = pl.ds(v * LANES, LANES)

            def coef(kind):
                return spread(coef_ref[coef_plane, kind : kind + 1, lanes])

            x_plus = ahead[v] if v == tiles - 1 else jnp.where(left, ahead[v], ahead[v + 1])
            x_minus = behind[v] if v == 0 else jnp.where(right, behind[v], behind[v - 1])
            total = centre[v] + coef(0) * source[plane + 1, at, lanes].astype(jnp.float32)
            side = coef(1) * source[plane - 1, at, lanes].astype(jnp.float32)
            total = total + coef(2) * pltpu.roll(centre[v], LANES - 1, 1)
            side = side + coef(3) * pltpu.roll(centre[v], 1, 1)
            total = total + coef(4) * x_plus
            side = side + coef(5) * x_minus
            return total + side

        return tile

    def relax_first(plane, at):
        sums = stencil(first, plane + 1, plane, at)
        base = (slab * depth + plane - 1) * cells
        mine = pl.ds(pl.multiple_of(pl.program_id(0) * rows + at.start, GROUP), GROUP)
        plus = elec_b[0, mine, :] - base
        minus = elec_b[1, mine, :] - base

        def tile(v):
            lanes = pl.ds(v * LANES, LANES)
            strength = spread(coef_ref[plane, 6:7, lanes])
            negative = spread(coef_ref[plane, 7:8, lanes])
            here = lane + v * LANES
            added = jnp.where(plus == here, strength, jnp.where(minus == here, negative, 0.0))
            extra[plane, at, lanes] = added
            second[plane, at, lanes] = sums(v) + added

        return tile

    def relax_second(plane, at):
        sums = stencil(second, plane + 1, plane + 1, at)

        def tile(v):
            lanes = pl.ds(v * LANES, LANES)
            value = sums(v) * (1.0 / 9.0) + extra[plane + 1, at, lanes] * (1.0 / 3.0)
            final[plane, at, lanes] = value.astype(jnp.bfloat16)

        return tile

    spans = [pl.ds(group * GROUP, GROUP) for group in range(groups)]

    def run(makers):
        works = [make() for make in makers]
        for v in range(tiles):
            for work in works:
                work(v)

    def only_first(plane, carry):
        for at in spans:
            run([lambda: relax_first(plane, at)])
        return carry

    def both(plane, carry):
        for at in spans:
            run([lambda: relax_second(plane - 3, at), lambda: relax_first(plane, at)])
        return carry

    planes = depth + 2
    lax.fori_loop(0, 3, only_first, 0)
    lax.fori_loop(3, planes, both, 0)
    for plane in range(planes - 3, depth):
        for at in spans:
            run([lambda: relax_second(plane, at)])
    pot_ref[...] = jnp.swapaxes(final[...].astype(jnp.float32), 0, 1).astype(jnp.bfloat16)

    wide = lane_index((rows, LANES))
    for r in range(count):
        out = outs[r]
        target = lax.rem(lax.axis_index("src") + r, count)
        start = pl.multiple_of(target * band, LANES)
        for plane in range(depth):
            out[:, plane * band : (plane + 1) * band] = final[plane, :, pl.ds(start, band)]
        after = jnp.minimum(target + 1, count - 1)
        after_start = pl.multiple_of(after * band, LANES)
        kept = (target < count - 1).astype(jnp.float32)
        for piece in range(beside_width(depth) // LANES):
            packed = jnp.zeros((rows, LANES), jnp.float32)
            for slot in range(LANES // NY):
                plane = piece * (LANES // NY) + slot
                if plane < depth:
                    row = final[plane, :, pl.ds(after_start, LANES)].astype(jnp.float32)
                    row = pltpu.roll(row, slot * NY, 1) if slot else row
                    mine = (wide >= slot * NY) & (wide < (slot + 1) * NY)
                    packed = jnp.where(mine, row, packed)
            begin = depth * band + piece * LANES
            out[:, begin : begin + LANES] = (packed * kept).astype(jnp.bfloat16)


def beside_width(depth):
    return -(-depth * NY // LANES) * LANES


def sweep(own, inner, outer, coefs, electrodes, before, total, begin, count, band):
    depth, size, cells = own.shape
    width = depth * band + beside_width(depth)
    block = begin // ROWS
    in_specs = [
        pl.BlockSpec((depth, ROWS, cells), lambda i: (0, i, 0)),
        pl.BlockSpec((HALO, ROWS, cells), lambda i: (0, i, 0)),
        pl.BlockSpec((HALO, ROWS, cells), lambda i: (0, i, 0)),
        pl.BlockSpec(coefs.shape, lambda i: (0, 0, 0)),
        pl.BlockSpec((2, UNIT), lambda i: (0, begin // UNIT)),
    ]
    args = [own, inner, outer, coefs, electrodes]
    aliases = {}
    if before is not None:
        in_specs.append(pl.BlockSpec(memory_space=pl.ANY))
        args.append(before)
        aliases = {5: 0}
    planes = depth + 2
    return pl.pallas_call(
        functools.partial(sweep_kernel, count, band),
        grid=(size // ROWS,),
        in_specs=in_specs,
        out_specs=[pl.BlockSpec((ROWS, depth, cells), lambda i: (i + block, 0, 0))]
        + [pl.BlockSpec((ROWS, width), lambda i: (i, 0))] * count,
        scratch_shapes=[
            pltpu.VMEM((2 * HALO + depth, ROWS, cells), jnp.bfloat16),
            pltpu.VMEM((planes, ROWS, cells), jnp.float32),
            pltpu.VMEM((planes, ROWS, cells), jnp.float32),
            pltpu.VMEM((depth, ROWS, cells), jnp.bfloat16),
            pltpu.VMEM((2, UNIT, LANES), jnp.int32),
        ],
        out_shape=[jax.ShapeDtypeStruct((total, depth, cells), jnp.bfloat16)]
        + [jax.ShapeDtypeStruct((size, width), jnp.bfloat16)] * count,
        input_output_aliases=aliases,
        compiler_params=pltpu.CompilerParams(vmem_limit_bytes=44 * 2**20),
        cost_estimate=pl.CostEstimate(
            flops=size * cells * planes * 40,
            bytes_accessed=size * cells * 2 * (3 * depth + 2 * HALO),
            transcendentals=0,
        ),
        name="sweep",
    )(*args)


def fold_kernel(count, per, weight_ref, out_ref):
    total = count * per

    def where_is(block):
        holder = lax.rem(lax.axis_index("src") + count - lax.rem(block, count), count)
        return pl.multiple_of((holder * per + lax.div(block, count)) * UNIT, UNIT)

    for q in range(total):
        here = where_is(q)
        rows = pl.ds(q * UNIT, UNIT)

        def folded(other, carry):
            there = where_is(other)
            straight = weight_ref[pl.ds(here, UNIT), pl.ds(there, UNIT)].astype(jnp.float32)
            turned = weight_ref[pl.ds(there, UNIT), pl.ds(here, UNIT)].astype(jnp.float32)
            columns = pl.ds(pl.multiple_of(other * UNIT, UNIT), UNIT)
            out_ref[rows, columns] = (straight + turned.T).astype(jnp.bfloat16)
            return carry

        if q:
            lax.fori_loop(0, q, folded, 0)
        out_ref[rows, q * UNIT : (q + 1) * UNIT] = weight_ref[pl.ds(here, UNIT), pl.ds(here, UNIT)]
        if q + 1 < total:
            rest = (UNIT, (total - q - 1) * UNIT)
            out_ref[rows, (q + 1) * UNIT :] = jnp.zeros(rest, jnp.bfloat16)


def fold(weight, count, per):
    return pl.pallas_call(
        functools.partial(fold_kernel, count, per),
        grid=(1,),
        in_specs=[pl.BlockSpec(weight.shape, lambda i: (0, 0))],
        out_specs=pl.BlockSpec(weight.shape, lambda i: (0, 0)),
        out_shape=jax.ShapeDtypeStruct(weight.shape, jnp.bfloat16),
        compiler_params=pltpu.CompilerParams(vmem_limit_bytes=16 * 2**20),
        cost_estimate=pl.CostEstimate(
            flops=weight.size, bytes_accessed=weight.size * 4, transcendentals=0
        ),
        name="fold",
    )(weight)


def weigh_kernel(depth, band, pieces, above, row_start, block_rows, scale, weight_ref, *refs):
    piece_refs, above_refs = refs[:pieces], refs[pieces : pieces + above]
    before_ref, out_ref, held, mixed, partial, sems = refs[pieces + above :]
    step = pl.program_id(0)
    tiles = band // LANES
    wide = depth * band + beside_width(depth)

    @pl.when(step == 0)
    def _():
        copies = []
        for group, column in ((piece_refs, 0), (above_refs, wide)):
            at = 0
            for ref in group:
                size, width = ref.shape
                into = held.at[pl.ds(at, size), pl.ds(column, width)]
                copies.append(pltpu.make_async_copy(ref, into, sems.at[len(copies)]))
                copies[-1].start()
                at += size
        for copy in copies:
            copy.wait()
        partial[...] = before_ref[...]

    for c in range(row_start // UNIT, held.shape[0] // UNIT):
        reach = (c + 1) * UNIT

        @pl.when(step == c - row_start // UNIT)
        def _():
            mixed[...] = jnp.dot(
                weight_ref[:, :reach], held[:reach], preferred_element_type=jnp.float32
            )

    lane = lane_index((GROUP, LANES))
    left = lane < LANES - NY
    inner = jnp.where(lax.rem(lane, NY) != NY - 1, 1.0, 0.0)
    base = row_start + step * block_rows

    for plane in range(depth):
        beside_tile = depth * band + (plane * NY // LANES) * LANES
        turn = (LANES - NY - plane * NY) % LANES

        def rows_of(group, totals):
            at = pl.ds(pl.multiple_of(group * GROUP, GROUP), GROUP)
            at_held = pl.ds(pl.multiple_of(base + group * GROUP, GROUP), GROUP)

            def read(column):
                lanes = pl.ds(column, LANES)
                return held[at_held, lanes].astype(jnp.float32), mixed[at, lanes]

            centre = [read(plane * band + t * LANES) for t in range(tiles)]
            over = (plane + 1) * band if plane < depth - 1 else wide
            above = [read(over + t * LANES) for t in range(tiles)]
            ahead = [tuple(pltpu.roll(c, LANES - NY, 1) for c in pair) for pair in centre]
            ahead.append(tuple(pltpu.roll(c, turn, 1) if turn else c for c in read(beside_tile)))
            result = []
            for t in range(tiles):
                value, product = centre[t]
                total = (above[t][0] - value) * (above[t][1] - product)
                total = total + (jnp.where(left, ahead[t][0], ahead[t + 1][0]) - value) * (
                    jnp.where(left, ahead[t][1], ahead[t + 1][1]) - product
                )
                total = total + (pltpu.roll(value, LANES - 1, 1) * inner - value) * (
                    pltpu.roll(product, LANES - 1, 1) * inner - product
                )
                result.append(totals[t] + (total[:8] + total[8:]))
            return tuple(result)

        rows = pl.ds(plane * 8, 8)
        start = tuple(partial[rows, t * LANES : (t + 1) * LANES] for t in range(tiles))
        sums = lax.fori_loop(0, block_rows // GROUP, rows_of, start, unroll=True)
        for t in range(tiles):
            partial[rows, t * LANES : (t + 1) * LANES] = sums[t]

    @pl.when(step == pl.num_programs(0) - 1)
    def _():
        if scale is None:
            out_ref[...] = partial[...]
        else:
            for plane in range(depth):
                total = jnp.sum(partial[plane * 8 : plane * 8 + 8, :], axis=0, keepdims=True)
                out_ref[plane : plane + 1, :] = total * scale


def weigh(weight, pieces, above, before, row_start, rows, depth, band, scale):
    width = pieces[0].shape[1] + band
    held = sum(piece.shape[0] for piece in pieces)
    block_rows = UNIT
    first = row_start // block_rows
    out = (depth, band) if scale is not None else (depth * 8, band)
    return pl.pallas_call(
        functools.partial(
            weigh_kernel, depth, band, len(pieces), len(above), row_start, block_rows, scale
        ),
        grid=(rows // block_rows,),
        in_specs=[pl.BlockSpec((block_rows, weight.shape[1]), lambda i: (i + first, 0))]
        + [pl.BlockSpec(memory_space=pl.ANY)] * (len(pieces) + len(above))
        + [pl.BlockSpec((depth * 8, band), lambda i: (0, 0))],
        out_specs=pl.BlockSpec(out, lambda i: (0, 0)),
        out_shape=jax.ShapeDtypeStruct(out, jnp.float32),
        scratch_shapes=[
            pltpu.VMEM((held, width), jnp.bfloat16),
            pltpu.VMEM((block_rows, width), jnp.float32),
            pltpu.VMEM((depth * 8, band), jnp.float32),
            pltpu.SemaphoreType.DMA((len(pieces) + len(above),)),
        ],
        compiler_params=pltpu.CompilerParams(vmem_limit_bytes=32 * 2**20),
        cost_estimate=pl.CostEstimate(
            flops=2 * rows * held * width, bytes_accessed=2 * held * width, transcendentals=0
        ),
        name="weigh",
    )(weight, *pieces, *above, before)


def body(conductivity, prev_fields, electrodes, data_weight):
    local, depth, cells = prev_fields.shape
    ends = electrodes.T
    count = lax.axis_size("src")
    band = cells // count
    sources = data_weight.shape[0]
    per = local // UNIT
    halos = []
    for k in range(per):
        own, inner, outer = pack(prev_fields, conductivity, k)
        outer = lax.ppermute(outer, "cells", pairs_of("cells", 1))
        inner = lax.ppermute(inner, "cells", pairs_of("cells", 0))
        halos.append((own, inner, outer))
    coefs = stencil_coefficients(conductivity, *halos[0][1:], depth * lax.axis_size("cells"))
    weight = fold(data_weight, count, per)
    down = [(i + 1, i) for i in range(lax.axis_size("cells") - 1)]
    stops = sorted({max(per - 2, 0) * count, (per - 1) * count + 1, per * count} - {0})
    potentials = None
    pieces, above = [], []
    sums = jnp.zeros((depth * 8, band), jnp.float32)
    done = 0
    for k in range(per):
        potentials, kept, *sent = sweep(
            *halos[k], coefs, ends, potentials, local, k * UNIT, count, band
        )
        pieces.append(kept)
        for r in range(1, count):
            pairs = [(i, (i + r) % count) for i in range(count)]
            pieces.append(lax.ppermute(sent[r - 1], "src", pairs))
    for stop in stops:
        lowest = jnp.concatenate([p[:, :band] for p in pieces[done:stop]], axis=0)
        above.append(lax.ppermute(lowest, "cells", down))
        sums = weigh(
            weight,
            pieces[:stop],
            above,
            sums,
            done * UNIT,
            (stop - done) * UNIT,
            depth,
            band,
            1.0 / sources if stop == per * count else None,
        )
        done = stop
    return (potentials, sums)


def solution(mesh):
    placed = (P("cells", None), P("src", "cells", None), P("src", None), P())
    return jax.shard_map(
        body,
        mesh=mesh,
        in_specs=placed,
        out_specs=(P("src", "cells", None), P("cells", "src")),
        check_vma=False,
    )
```

```python
import functools

import jax
import jax.numpy as jnp
from jax import lax
from jax.experimental import pallas as pl
from jax.experimental.pallas import tpu as pltpu
from jax.sharding import PartitionSpec as P


NY = 32
current = 4.0
LANES = 128
GROUP = 16
ROWS = 64
UNIT = 128
HALO = 2
PART = 8


def pairs_of(axis, first):
    count = lax.axis_size(axis)
    pairs = [(i, i + 1) for i in range(first, count - 1, 2)]
    return pairs + [(b, a) for a, b in pairs]


def coefficient_kernel(depth, planes_total, sigma_ref, inner_ref, outer_ref, out_ref, padded):
    cells = sigma_ref.shape[1]
    planes = depth + 2
    slab = lax.axis_index("cells")
    odd = lax.rem(slab, 2)

    def put(at, ref):
        for i in range(HALO):
            part = ref[i].astype(jnp.float32)
            padded[at + i : at + i + 1, :] = (part[2:3] + part[1:2]) + part[0:1]

    padded[HALO : HALO + depth, :] = sigma_ref[...]

    @pl.when(odd == 0)
    def _():
        put(0, outer_ref)
        put(HALO + depth, inner_ref)

    @pl.when(odd == 1)
    def _():
        put(0, inner_ref)
        put(HALO + depth, outer_ref)

    sigma = padded[1 : planes + 1, :]
    column = lax.broadcasted_iota(jnp.int32, sigma.shape, 1)
    row = lax.rem(column, NY)
    plane = slab * depth - 1 + lax.broadcasted_iota(jnp.int32, sigma.shape, 0)
    inside = (plane >= 0) & (plane < planes_total)
    zero = jnp.zeros_like(sigma)
    upper, lower = row != NY - 1, row != 0
    ahead, behind = column < cells - NY, column >= NY
    z_plus = 0.5 * (sigma + padded[2 : planes + 2, :])
    z_minus = 0.5 * (sigma + padded[0:planes, :])
    y_plus = 0.5 * (sigma + jnp.where(upper, pltpu.roll(sigma, cells - 1, 1), zero))
    y_minus = 0.5 * (sigma + jnp.where(lower, pltpu.roll(sigma, 1, 1), zero))
    x_plus = 0.5 * (sigma + jnp.where(ahead, pltpu.roll(sigma, cells - NY, 1), zero))
    x_minus = 0.5 * (sigma + jnp.where(behind, pltpu.roll(sigma, NY, 1), zero))
    diagonal = z_plus + z_minus + y_plus + y_minus + x_plus + x_minus
    scale = jnp.where(inside, 2.0 / jnp.where(inside, diagonal, 1.0), zero)
    kinds = [
        z_plus * scale,
        z_minus * scale,
        jnp.where(upper, y_plus * scale, zero),
        jnp.where(lower, y_minus * scale, zero),
        jnp.where(ahead, x_plus * scale, zero),
        jnp.where(behind, x_minus * scale, zero),
        current * scale,
        -current * scale,
    ]
    for kind, values in enumerate(kinds):
        for i in range(planes):
            out_ref[i, kind : kind + 1, :] = values[i : i + 1, :]


def stencil_coefficients(conductivity, inner, outer, planes_total):
    depth, cells = conductivity.shape
    part = inner.shape[1] // PART - 1
    shape = (depth + 2, 8, cells)
    return pl.pallas_call(
        functools.partial(coefficient_kernel, depth, planes_total),
        grid=(1,),
        in_specs=[pl.BlockSpec((depth, cells), lambda i: (0, 0))]
        + [pl.BlockSpec((HALO, PART, cells), lambda i: (0, part, 0))] * 2,
        out_specs=pl.BlockSpec(shape, lambda i: (0, 0, 0)),
        out_shape=jax.ShapeDtypeStruct(shape, jnp.float32),
        scratch_shapes=[pltpu.VMEM((2 * HALO + depth, cells), jnp.float32)],
        compiler_params=pltpu.CompilerParams(vmem_limit_bytes=8 * 2**20),
        name="coefficients",
    )(conductivity, inner, outer)


def pack_kernel(extra, fields_ref, sigma_ref, own_ref, inner_ref, outer_ref):
    rows, depth, cells = fields_ref.shape
    odd = lax.rem(lax.axis_index("cells"), 2)
    own_ref[...] = jnp.swapaxes(fields_ref[...].astype(jnp.float32), 0, 1).astype(jnp.bfloat16)

    def part(plane):
        rest = jnp.broadcast_to(sigma_ref[plane : plane + 1, :], (PART, cells))
        row = lax.broadcasted_iota(jnp.int32, rest.shape, 0)
        parts = jnp.zeros_like(rest)
        for i in range(3):
            rounded = rest.astype(jnp.bfloat16).astype(jnp.float32)
            parts = jnp.where(row == i, rounded, parts)
            rest = rest - rounded
        return parts.astype(jnp.bfloat16)

    def pick(out_ref, start):
        out_ref[:, 0:rows] = own_ref[start : start + HALO]
        if extra:
            for i in range(HALO):
                out_ref[i, rows : rows + PART, :] = part(start + i)

    @pl.when(odd == 0)
    def _():
        pick(inner_ref, depth - HALO)
        pick(outer_ref, 0)

    @pl.when(odd == 1)
    def _():
        pick(inner_ref, 0)
        pick(outer_ref, depth - HALO)


def pack(fields, conductivity, k):
    _, depth, cells = fields.shape
    extra = k == 0
    rows = UNIT
    steps = UNIT // rows
    sent = UNIT + (PART if extra else 0)
    block = sent
    return pl.pallas_call(
        functools.partial(pack_kernel, extra),
        grid=(steps,),
        in_specs=[
            pl.BlockSpec((rows, depth, cells), lambda i: (i + k * steps, 0, 0)),
            pl.BlockSpec((depth, cells), lambda i: (0, 0)),
        ],
        out_specs=[pl.BlockSpec((depth, rows, cells), lambda i: (0, i, 0))]
        + [pl.BlockSpec((HALO, block, cells), lambda i: (0, i, 0))] * 2,
        out_shape=[jax.ShapeDtypeStruct((depth, UNIT, cells), jnp.bfloat16)]
        + [jax.ShapeDtypeStruct((HALO, sent, cells), jnp.bfloat16)] * 2,
        compiler_params=pltpu.CompilerParams(vmem_limit_bytes=60 * 2**20),
        name="pack",
    )(fields, conductivity)


def lane_index(shape):
    return lax.broadcasted_iota(jnp.int32, shape, 1)


def sweep_kernel(count, band, own_ref, inner_ref, outer_ref, coef_ref, elec_ref, *refs):
    refs = refs[-(count + 6) :]
    pot_ref, outs, (first, second, extra, final) = refs[0], refs[1 : count + 1], refs[count + 1 : count + 5]
    elec_b = refs[count + 5]
    depth, rows, cells = own_ref.shape
    slab = lax.axis_index("cells")
    odd = lax.rem(slab, 2)
    tiles = cells // LANES
    first[HALO : HALO + depth] = own_ref[...]

    @pl.when(odd == 0)
    def _():
        first[0:HALO] = outer_ref[...]
        first[HALO + depth :] = inner_ref[...]

    @pl.when(odd == 1)
    def _():
        first[0:HALO] = inner_ref[...]
        first[HALO + depth :] = outer_ref[...]


    @pl.when(pl.program_id(0) == 0)
    def _():
        for e in range(2):
            line = jnp.broadcast_to(elec_ref[e : e + 1, :].astype(jnp.float32), (LANES, UNIT))
            elec_b[e] = line.T.astype(jnp.int32)

    lane = lane_index((GROUP, LANES))
    left = lane < LANES - NY
    right = lane >= NY
    groups = rows // GROUP

    def spread(row):
        return jnp.broadcast_to(row, (GROUP, LANES))

    def stencil(source, plane, coef_plane, at):
        centre = [source[plane, at, pl.ds(v * LANES, LANES)].astype(jnp.float32) for v in range(tiles)]
        ahead = [pltpu.roll(c, LANES - NY, 1) for c in centre]
        behind = [pltpu.roll(c, NY, 1) for c in centre]

        def tile(v):
            lanes = pl.ds(v * LANES, LANES)

            def coef(kind):
                return spread(coef_ref[coef_plane, kind : kind + 1, lanes])

            x_plus = ahead[v] if v == tiles - 1 else jnp.where(left, ahead[v], ahead[v + 1])
            x_minus = behind[v] if v == 0 else jnp.where(right, behind[v], behind[v - 1])
            total = centre[v] + coef(0) * source[plane + 1, at, lanes].astype(jnp.float32)
            side = coef(1) * source[plane - 1, at, lanes].astype(jnp.float32)
            total = total + coef(2) * pltpu.roll(centre[v], LANES - 1, 1)
            side = side + coef(3) * pltpu.roll(centre[v], 1, 1)
            total = total + coef(4) * x_plus
            side = side + coef(5) * x_minus
            return total + side

        return tile

    def relax_first(plane, at):
        sums = stencil(first, plane + 1, plane, at)
        base = (slab * depth + plane - 1) * cells
        mine = pl.ds(pl.multiple_of(pl.program_id(0) * rows + at.start, GROUP), GROUP)
        plus = elec_b[0, mine, :] - base
        minus = elec_b[1, mine, :] - base

        def tile(v):
            lanes = pl.ds(v * LANES, LANES)
            strength = spread(coef_ref[plane, 6:7, lanes])
            negative = spread(coef_ref[plane, 7:8, lanes])
            here = lane + v * LANES
            added = jnp.where(plus == here, strength, jnp.where(minus == here, negative, 0.0))
            extra[plane, at, lanes] = added
            second[plane, at, lanes] = sums(v) + added

        return tile

    def relax_second(plane, at):
        sums = stencil(second, plane + 1, plane + 1, at)

        def tile(v):
            lanes = pl.ds(v * LANES, LANES)
            value = sums(v) * (1.0 / 9.0) + extra[plane + 1, at, lanes] * (1.0 / 3.0)
            final[plane, at, lanes] = value.astype(jnp.bfloat16)

        return tile

    spans = [pl.ds(group * GROUP, GROUP) for group in range(groups)]

    def run(makers):
        works = [make() for make in makers]
        for v in range(tiles):
            for work in works:
                work(v)

    def only_first(plane, carry):
        for at in spans:
            run([lambda: relax_first(plane, at)])
        return carry

    def both(plane, carry):
        for at in spans:
            run([lambda: relax_second(plane - 3, at), lambda: relax_first(plane, at)])
        return carry

    planes = depth + 2
    lax.fori_loop(0, 3, only_first, 0)
    lax.fori_loop(3, planes, both, 0)
    for plane in range(planes - 3, depth):
        for at in spans:
            run([lambda: relax_second(plane, at)])
    pot_ref[...] = jnp.swapaxes(final[...].astype(jnp.float32), 0, 1).astype(jnp.bfloat16)

    wide = lane_index((rows, LANES))
    for r in range(count):
        out = outs[r]
        target = lax.rem(lax.axis_index("src") + r, count)
        start = pl.multiple_of(target * band, LANES)
        for plane in range(depth):
            out[:, plane * band : (plane + 1) * band] = final[plane, :, pl.ds(start, band)]
        after = jnp.minimum(target + 1, count - 1)
        after_start = pl.multiple_of(after * band, LANES)
        kept = (target < count - 1).astype(jnp.float32)
        for piece in range(beside_width(depth) // LANES):
            packed = jnp.zeros((rows, LANES), jnp.float32)
            for slot in range(LANES // NY):
                plane = piece * (LANES // NY) + slot
                if plane < depth:
                    row = final[plane, :, pl.ds(after_start, LANES)].astype(jnp.float32)
                    row = pltpu.roll(row, slot * NY, 1) if slot else row
                    mine = (wide >= slot * NY) & (wide < (slot + 1) * NY)
                    packed = jnp.where(mine, row, packed)
            begin = depth * band + piece * LANES
            out[:, begin : begin + LANES] = (packed * kept).astype(jnp.bfloat16)


def beside_width(depth):
    return -(-depth * NY // LANES) * LANES


def sweep(own, inner, outer, coefs, electrodes, before, total, begin, count, band):
    depth, size, cells = own.shape
    width = depth * band + beside_width(depth)
    block = begin // ROWS
    in_specs = [
        pl.BlockSpec((depth, ROWS, cells), lambda i: (0, i, 0)),
        pl.BlockSpec((HALO, ROWS, cells), lambda i: (0, i, 0)),
        pl.BlockSpec((HALO, ROWS, cells), lambda i: (0, i, 0)),
        pl.BlockSpec(coefs.shape, lambda i: (0, 0, 0)),
        pl.BlockSpec((2, UNIT), lambda i: (0, begin // UNIT)),
    ]
    args = [own, inner, outer, coefs, electrodes]
    aliases = {}
    if before is not None:
        in_specs.append(pl.BlockSpec(memory_space=pl.ANY))
        args.append(before)
        aliases = {5: 0}
    planes = depth + 2
    return pl.pallas_call(
        functools.partial(sweep_kernel, count, band),
        grid=(size // ROWS,),
        in_specs=in_specs,
        out_specs=[pl.BlockSpec((ROWS, depth, cells), lambda i: (i + block, 0, 0))]
        + [pl.BlockSpec((ROWS, width), lambda i: (i, 0))] * count,
        scratch_shapes=[
            pltpu.VMEM((2 * HALO + depth, ROWS, cells), jnp.bfloat16),
            pltpu.VMEM((planes, ROWS, cells), jnp.float32),
            pltpu.VMEM((planes, ROWS, cells), jnp.float32),
            pltpu.VMEM((depth, ROWS, cells), jnp.bfloat16),
            pltpu.VMEM((2, UNIT, LANES), jnp.int32),
        ],
        out_shape=[jax.ShapeDtypeStruct((total, depth, cells), jnp.bfloat16)]
        + [jax.ShapeDtypeStruct((size, width), jnp.bfloat16)] * count,
        input_output_aliases=aliases,
        compiler_params=pltpu.CompilerParams(vmem_limit_bytes=44 * 2**20),
        cost_estimate=pl.CostEstimate(
            flops=size * cells * planes * 40,
            bytes_accessed=size * cells * 2 * (3 * depth + 2 * HALO),
            transcendentals=0,
        ),
        name="sweep",
    )(*args)


def fold_kernel(count, per, weight_ref, out_ref):
    total = count * per

    def where_is(block):
        holder = lax.rem(lax.axis_index("src") + count - lax.rem(block, count), count)
        return pl.multiple_of((holder * per + lax.div(block, count)) * UNIT, UNIT)

    for q in range(total):
        here = where_is(q)
        rows = pl.ds(q * UNIT, UNIT)

        def folded(other, carry):
            there = where_is(other)
            straight = weight_ref[pl.ds(here, UNIT), pl.ds(there, UNIT)].astype(jnp.float32)
            turned = weight_ref[pl.ds(there, UNIT), pl.ds(here, UNIT)].astype(jnp.float32)
            columns = pl.ds(pl.multiple_of(other * UNIT, UNIT), UNIT)
            out_ref[rows, columns] = (straight + turned.T).astype(jnp.bfloat16)
            return carry

        if q:
            lax.fori_loop(0, q, folded, 0)
        out_ref[rows, q * UNIT : (q + 1) * UNIT] = weight_ref[pl.ds(here, UNIT), pl.ds(here, UNIT)]
        if q + 1 < total:
            rest = (UNIT, (total - q - 1) * UNIT)
            out_ref[rows, (q + 1) * UNIT :] = jnp.zeros(rest, jnp.bfloat16)


def fold(weight, count, per):
    return pl.pallas_call(
        functools.partial(fold_kernel, count, per),
        grid=(1,),
        in_specs=[pl.BlockSpec(weight.shape, lambda i: (0, 0))],
        out_specs=pl.BlockSpec(weight.shape, lambda i: (0, 0)),
        out_shape=jax.ShapeDtypeStruct(weight.shape, jnp.bfloat16),
        compiler_params=pltpu.CompilerParams(vmem_limit_bytes=16 * 2**20),
        cost_estimate=pl.CostEstimate(
            flops=weight.size, bytes_accessed=weight.size * 4, transcendentals=0
        ),
        name="fold",
    )(weight)


def weigh_kernel(depth, band, pieces, above, row_start, block_rows, scale, weight_ref, *refs):
    piece_refs, above_refs = refs[:pieces], refs[pieces : pieces + above]
    before_ref, out_ref, held, mixed, partial, sems = refs[pieces + above :]
    step = pl.program_id(0)
    tiles = band // LANES
    wide = depth * band + beside_width(depth)

    @pl.when(step == 0)
    def _():
        copies = []
        for group, column in ((piece_refs, 0), (above_refs, wide)):
            at = 0
            for ref in group:
                size, width = min(ref.shape[0], held.shape[0] - at), ref.shape[1]
                if size <= 0:
                    continue
                into = held.at[pl.ds(at, size), pl.ds(column, width)]
                copies.append(pltpu.make_async_copy(ref.at[pl.ds(0, size)], into, sems.at[len(copies)]))
                copies[-1].start()
                at += size
        for copy in copies:
            copy.wait()
        partial[...] = before_ref[...]

    for c in range(row_start // UNIT, held.shape[0] // UNIT):
        reach = (c + 1) * UNIT

        @pl.when(step == c - row_start // UNIT)
        def _():
            mixed[...] = jnp.dot(
                weight_ref[:, :reach], held[:reach], preferred_element_type=jnp.float32
            )

    lane = lane_index((GROUP, LANES))
    left = lane < LANES - NY
    inner = jnp.where(lax.rem(lane, NY) != NY - 1, 1.0, 0.0)
    base = row_start + step * block_rows

    for plane in range(depth):
        beside_tile = depth * band + (plane * NY // LANES) * LANES
        turn = (LANES - NY - plane * NY) % LANES

        def rows_of(group, totals):
            at = pl.ds(pl.multiple_of(group * GROUP, GROUP), GROUP)
            at_held = pl.ds(pl.multiple_of(base + group * GROUP, GROUP), GROUP)

            def read(column):
                lanes = pl.ds(column, LANES)
                return held[at_held, lanes].astype(jnp.float32), mixed[at, lanes]

            centre = [read(plane * band + t * LANES) for t in range(tiles)]
            over = (plane + 1) * band if plane < depth - 1 else wide
            above = [read(over + t * LANES) for t in range(tiles)]
            ahead = [tuple(pltpu.roll(c, LANES - NY, 1) for c in pair) for pair in centre]
            ahead.append(tuple(pltpu.roll(c, turn, 1) if turn else c for c in read(beside_tile)))
            result = []
            for t in range(tiles):
                value, product = centre[t]
                total = (above[t][0] - value) * (above[t][1] - product)
                total = total + (jnp.where(left, ahead[t][0], ahead[t + 1][0]) - value) * (
                    jnp.where(left, ahead[t][1], ahead[t + 1][1]) - product
                )
                total = total + (pltpu.roll(value, LANES - 1, 1) * inner - value) * (
                    pltpu.roll(product, LANES - 1, 1) * inner - product
                )
                result.append(totals[t] + (total[:8] + total[8:]))
            return tuple(result)

        rows = pl.ds(plane * 8, 8)
        start = tuple(partial[rows, t * LANES : (t + 1) * LANES] for t in range(tiles))
        sums = lax.fori_loop(0, block_rows // GROUP, rows_of, start, unroll=True)
        for t in range(tiles):
            partial[rows, t * LANES : (t + 1) * LANES] = sums[t]

    @pl.when(step == pl.num_programs(0) - 1)
    def _():
        if scale is None:
            out_ref[...] = partial[...]
        else:
            for plane in range(depth):
                total = jnp.sum(partial[plane * 8 : plane * 8 + 8, :], axis=0, keepdims=True)
                out_ref[plane : plane + 1, :] = total * scale


def weigh(weight, pieces, above, before, row_start, rows, depth, band, scale):
    width = pieces[0].shape[1] + band
    held = sum(piece.shape[0] for piece in pieces)
    block_rows = UNIT
    first = row_start // block_rows
    out = (depth, band) if scale is not None else (depth * 8, band)
    return pl.pallas_call(
        functools.partial(
            weigh_kernel, depth, band, len(pieces), len(above), row_start, block_rows, scale
        ),
        grid=(rows // block_rows,),
        in_specs=[pl.BlockSpec((block_rows, weight.shape[1]), lambda i: (i + first, 0))]
        + [pl.BlockSpec(memory_space=pl.ANY)] * (len(pieces) + len(above))
        + [pl.BlockSpec((depth * 8, band), lambda i: (0, 0))],
        out_specs=pl.BlockSpec(out, lambda i: (0, 0)),
        out_shape=jax.ShapeDtypeStruct(out, jnp.float32),
        scratch_shapes=[
            pltpu.VMEM((held, width), jnp.bfloat16),
            pltpu.VMEM((block_rows, width), jnp.float32),
            pltpu.VMEM((depth * 8, band), jnp.float32),
            pltpu.SemaphoreType.DMA((len(pieces) + len(above),)),
        ],
        compiler_params=pltpu.CompilerParams(vmem_limit_bytes=32 * 2**20),
        cost_estimate=pl.CostEstimate(
            flops=2 * rows * held * width, bytes_accessed=2 * held * width, transcendentals=0
        ),
        name="weigh",
    )(weight, *pieces, *above, before)


def body(conductivity, prev_fields, electrodes, data_weight):
    local, depth, cells = prev_fields.shape
    ends = electrodes.T
    count = lax.axis_size("src")
    band = cells // count
    sources = data_weight.shape[0]
    per = local // UNIT
    halos = []
    for k in range(per):
        own, inner, outer = pack(prev_fields, conductivity, k)
        outer = lax.ppermute(outer, "cells", pairs_of("cells", 1))
        inner = lax.ppermute(inner, "cells", pairs_of("cells", 0))
        halos.append((own, inner, outer))
    coefs = stencil_coefficients(conductivity, *halos[0][1:], depth * lax.axis_size("cells"))
    weight = fold(data_weight, count, per)
    down = [(i + 1, i) for i in range(lax.axis_size("cells") - 1)]
    stops = sorted({max(per - 2, 0) * count, (per - 1) * count, (per - 1) * count + 1, per * count} - {0})
    shared = {(per - 1) * count: (per - 1) * count + 1}
    potentials = None
    pieces, above = [], []
    sums = jnp.zeros((depth * 8, band), jnp.float32)
    done = 0
    for k in range(per):
        potentials, kept, *sent = sweep(
            *halos[k], coefs, ends, potentials, local, k * UNIT, count, band
        )
        pieces.append(kept)
        for r in range(1, count):
            pairs = [(i, (i + r) % count) for i in range(count)]
            pieces.append(lax.ppermute(sent[r - 1], "src", pairs))
    covered = 0
    for stop in stops:
        if covered < stop:
            end = shared.get(stop, stop)
            lowest = jnp.concatenate([p[:, :band] for p in pieces[covered:end]], axis=0)
            above.append(lax.ppermute(lowest, "cells", down))
            covered = end
        sums = weigh(
            weight,
            pieces[:stop],
            above,
            sums,
            done * UNIT,
            (stop - done) * UNIT,
            depth,
            band,
            1.0 / sources if stop == per * count else None,
        )
        done = stop
    return (potentials, sums)


def solution(mesh):
    placed = (P("cells", None), P("src", "cells", None), P("src", None), P())
    return jax.shard_map(
        body,
        mesh=mesh,
        in_specs=placed,
        out_specs=(P("src", "cells", None), P("cells", "src")),
        check_vma=False,
    )
```
